32 devices in a mesh: groups: 2 (over y), seq: 4 (over z), dp: 2 (over x), mp: 2 (over core).
Axes of the slice: x: 2, y: 2, z: 4, core: 2. Of those that a mesh axis runs over, the one named last changes fastest.
Arguments:
- tiles: bfloat16 [160, 8, 8, 768], P(('groups', 'seq', 'dp')), parts along dimension 0, may hold values from -6 to 6
- token_grad: bfloat16 [160, 8, 8, 768], P(('groups', 'seq', 'dp')), parts along dimension 0, may hold values from -1.5 to 1.5
- embed_grad: bfloat16 [2, 80, 768], P('dp', 'groups', 'seq'), parts along dimension 1, may hold values from -48 to 48
- live_tiles: int32 [16], P(('groups', 'seq', 'dp')), parts along dimension 0, may hold values from 1 to 10, 60 in all
- dw_kernel: float32 [7, 7, 768], replicated, may hold values from -0.875 to 0.875
- dw_bias: float32 [768], replicated, may hold values from -3 to 3
- ln_gain: float32 [768], replicated, may hold values from 0.1 to 1.9
- ln_bias: float32 [768], replicated, may hold values from -2 to 2
- w_up: bfloat16 [768, 2560], P('seq', 'mp'), may hold values from -0.21875 to 0.21875
- b_up: float32 [2560], P('mp'), may hold values from -3 to 3
- w_down: bfloat16 [768, 2560], P('seq', 'mp'), may hold values from -0.125 to 0.125
- layer_scale: float32 [768], replicated, may hold values from 0.3 to 1.5
Outputs:
- tile_grad: bfloat16 [160, 8, 8, 768], P(('groups', 'seq', 'dp')), parts along dimension 0
- grad_up: float32 [1536, 2560], P(('groups', 'seq'), 'mp'), parts along dimension 0
- grad_down: float32 [1536, 2560], P(('groups', 'seq'), 'mp'), parts along dimension 0
The draws below stay inside these ranges and needn't reach their ends.
There are 2 independent parts, one for each index of `groups`. The reference program is written for one: setup_inputs(seed, part) draws one part's arguments, and reference() takes and returns one part's arrays. A program takes and returns all parts, laid end to end along the dimension named above; an argument that names none is the same for every part. Nothing has to cross between parts.
Inputs may be any that keep to these rules, and one draw needn't show every extreme that they name: Each loader's foreground tiles fill its slots 0 to live_tiles - 1 of 10; some loader has all 10.
All inputs are finite; a program needn't handle non-finite values. No bound on the sum of `live_tiles` on one device may be relied on, other than what follows from the above.
Results may differ from the reference program's by a relative error of at most 0.01.
Values may be sent and summed in bfloat16 or wider, within the bound.
No kernel may reach another device: no remote copies, remote signals or barrier semaphores. Data moves between devices by JAX's collectives and lax.ppermute only.
A program may use at most 64 MiB of HBM per device.

```python
import math
import jax
import jax.numpy as jnp
import numpy as np
from jax import lax

DIM = 768
HIDDEN_SIZE = 2560
MAP = 8
KERNEL = 7
TILE_DEV = 10
OWNERS = 8
TILES = 80
N_SEQ = 4
N_DP = 2


def spiked(result, key, source, target, blocks, factor):
    def block_of(axis_at):
        return (jnp.arange(result.shape[axis_at]) // (result.shape[axis_at] // blocks)).reshape((-1,) + (1,) * (result.ndim - 1 - axis_at))

    one_side = jax.random.permutation(key, blocks)[block_of(target)]
    second = (block_of(target) + blocks // 2) % blocks
    return jnp.where((block_of(source) == one_side) | (block_of(source) == second), factor * result, result)


def level_of(key, shape, pieces, smallest, largest):
    gain, own = 1.0, jax.random.fold_in(key, 6)
    for dim, blocks in pieces:
        steps = jnp.exp(jax.random.uniform(jax.random.fold_in(own, dim), (blocks,), jnp.float32, smallest / len(pieces), largest / len(pieces)))
        gain = gain * jnp.repeat(steps, shape[dim] // blocks).reshape([-1 if axis == dim else 1 for axis in range(len(shape))])
    return gain


def split_up(number_of, total, most, slope):
    loads = [(1 << 20) // math.isqrt(grade ** slope) + 1 for grade in range(2, number_of + 1)]
    surplus, counts = total - most - (number_of - 1), [1] * (number_of - 1)
    while surplus > 0:
        movable = [i for i in range(number_of - 1) if counts[i] < most]
        pool, budget = sum([loads[i] for i in movable]), surplus
        for i in movable:
            extra = min(most - counts[i], max(1, budget * loads[i] // pool), surplus)
            counts[i] = counts[i] + extra
            surplus = surplus - extra
    return np.array([most] + counts)


def ragged_sizes(stream_key, number_of, total, most, skew):
    if number_of == 2:
        one = jax.random.randint(stream_key, (), max(1, total - most), min(most, total - 1) + 1)
        return jnp.stack([one, total - one])
    sizes = jnp.asarray(split_up(number_of, total, most, skew), jnp.int32)
    pairs = (number_of - 1) // 2
    giver, receiver = sizes[1:1 + 2 * pairs:2], sizes[2:2 + 2 * pairs:2]
    room = jnp.minimum(giver - 1, most - receiver)
    moved = jax.random.randint(jax.random.fold_in(stream_key, 1), (pairs,), 0, 1 << 20) % (room + 1)
    sizes = sizes.at[1:1 + 2 * pairs:2].set(giver - moved).at[2:2 + 2 * pairs:2].set(receiver + moved)
    return sizes[jax.random.permutation(jax.random.fold_in(stream_key, 2), number_of)]


def bell_draw(rng, dims, scale, limit, split=(), dtype=jnp.bfloat16):
    gain = level_of(rng, dims, split, -0.22, 0.18) if split else 1.0
    array = jax.random.normal(rng, dims, jnp.float32) * scale * gain
    return jnp.minimum(jnp.maximum(array, -limit), limit).astype(dtype)


def noise_with(key, shape, scale, most, pieces, heavy, held_as=jnp.bfloat16):
    drawn = scale * jax.random.normal(key, shape, jnp.float32)
    if pieces:
        drawn = drawn * level_of(key, shape, pieces, -0.22, 0.18)
    return jnp.clip(spiked(drawn, jax.random.fold_in(key, 3), *heavy), -most, most).astype(held_as)


def setup_inputs(seed: int = 0, part: int = 0) -> dict:
    key_list = jax.random.split(jax.random.key(seed), 13)
    own_keys = jax.random.split(jax.random.fold_in(key_list[12], part), 13)
    return {
        "tiles": bell_draw(own_keys[0], (TILES, MAP, MAP, DIM), 1.0, 6.0, ((0, 8),)),
        "token_grad": noise_with(own_keys[1], (TILES, MAP, MAP, DIM), 0.25, 1.5, ((0, 8),), (0, 3, 8, 2.0)),
        "embed_grad": bell_draw(own_keys[2], (N_DP, N_SEQ * TILE_DEV, DIM), 8.0, 48.0, ((0, 2), (2, 4))),
        "live_tiles": ragged_sizes(own_keys[3], OWNERS, OWNERS * TILE_DEV * 3 // 4, TILE_DEV, 2).astype(jnp.int32),
        "dw_kernel": bell_draw(key_list[4], (KERNEL, KERNEL, DIM), (KERNEL * KERNEL) ** -0.5, 0.875, (), jnp.float32),
        "dw_bias": bell_draw(key_list[5], (DIM,), 0.5, 3.0, (), jnp.float32),
        "ln_gain": jnp.clip(1.0 + 0.18 * jax.random.normal(key_list[6], (DIM,), jnp.float32), 0.1, 1.9),
        "ln_bias": bell_draw(key_list[7], (DIM,), 0.3, 2.0, (), jnp.float32),
        "w_up": bell_draw(key_list[8], (DIM, HIDDEN_SIZE), DIM ** -0.5, 0.21875, ((0, 4), (1, 2))),
        "b_up": bell_draw(key_list[9], (HIDDEN_SIZE,), 0.5, 3.0, ((0, 2),), jnp.float32),
        "w_down": bell_draw(key_list[10], (DIM, HIDDEN_SIZE), HIDDEN_SIZE ** -0.5, 0.125, ((0, 4), (1, 2))),
        "layer_scale": jnp.clip(jnp.exp(jax.random.uniform(key_list[11], (DIM,), jnp.float32, math.log(0.3), math.log(1.5))), 0.3, 1.5),
    }


sqrt_two_pi = 0.7978845608028654
cubic_coef = 0.044715

def depthwise(values, kernel):
    reach = kernel.shape[0]
    margin = reach // 2
    height = values.shape[1]
    padded = jnp.pad(values, ((0, 0), (margin, margin), (margin, margin), (0, 0)))
    total = jnp.zeros(values.shape, jnp.float32)
    for row_off in range(reach):
        for col_off in range(reach):
            total = total + padded[:, row_off:row_off + height, col_off:col_off + height, :] * kernel[row_off, col_off]
    return total

def gelu_tanh(values):
    inner = sqrt_two_pi * (values + cubic_coef * values * values * values)
    return 0.5 * values * (1.0 + jnp.tanh(inner))

def gelu_slope(values):
    tangent = jnp.tanh(sqrt_two_pi * (values + cubic_coef * values * values * values))
    return 0.5 * (1.0 + tangent) + 0.5 * values * (1.0 - tangent * tangent) * sqrt_two_pi * (1.0 + 3.0 * cubic_coef * values * values)

def normalize(values):
    center = lax.optimization_barrier(jnp.mean(values, axis=-1, keepdims=True))
    shifted = values - center
    spread = jnp.sqrt(lax.optimization_barrier(jnp.mean(shifted * shifted, axis=-1, keepdims=True)) + 1e-06)
    return (shifted / spread, spread)

def reference(tiles, token_grad, embed_grad, live_tiles, dw_kernel, dw_bias, ln_gain, ln_bias, w_up, b_up, w_down, layer_scale):
    width = tiles.shape[3]
    height = tiles.shape[1]
    owners = N_SEQ * N_DP
    tile_groups = tiles.reshape(owners, TILE_DEV, height, height, width)
    token_groups = token_grad.reshape(owners, TILE_DEV, height, height, width)
    pooled_groups = embed_grad.reshape(N_DP, N_SEQ, TILE_DEV, width).transpose(1, 0, 2, 3).reshape(owners, TILE_DEV, width)
    flipped = dw_kernel[::-1, ::-1, :]

    def owner_pass(carry, items):
        own_tiles, own_tokens, own_pooled, own_live = items
        conv = depthwise(own_tiles.astype(jnp.float32), dw_kernel) + dw_bias
        normal, spread = normalize(conv)
        normed = (normal * ln_gain + ln_bias).astype(jnp.bfloat16)
        rows = normed.reshape(-1, width)
        hidden = jnp.dot(rows, w_up, preferred_element_type=jnp.float32) + b_up
        act = gelu_tanh(hidden).astype(jnp.bfloat16)
        live = (jnp.arange(TILE_DEV) < own_live).astype(jnp.float32)[:, None, None, None]
        pooled = own_pooled.astype(jnp.float32)[:, None, None, :] * live
        out_grad = live * own_tokens.astype(jnp.float32) + pooled / (height * height)
        branch_grad = (layer_scale * out_grad).astype(jnp.bfloat16).reshape(-1, width)
        part_down = jnp.dot(branch_grad.T, act, preferred_element_type=jnp.float32).astype(jnp.bfloat16)
        act_grad = jnp.dot(branch_grad, w_down, preferred_element_type=jnp.float32)
        hidden_grad = (act_grad * gelu_slope(hidden)).astype(jnp.bfloat16)
        part_up = jnp.dot(rows.T, hidden_grad, preferred_element_type=jnp.float32).astype(jnp.bfloat16)
        normed_grad = jnp.dot(hidden_grad, w_up.T, preferred_element_type=jnp.float32)
        scaled = normed_grad.reshape(conv.shape) * ln_gain
        conv_grad = (scaled - lax.optimization_barrier(jnp.mean(scaled, axis=-1, keepdims=True)) - normal * lax.optimization_barrier(jnp.mean(scaled * normal, axis=-1, keepdims=True))) / spread
        input_grad = (out_grad + depthwise(conv_grad, flipped)).astype(jnp.bfloat16)
        carry = (carry[0] + part_up.astype(jnp.float32), carry[1] + part_down.astype(jnp.float32))
        return (carry, input_grad)
    start = (jnp.zeros(w_up.shape, jnp.float32), jnp.zeros(w_down.shape, jnp.float32))
    totals, grads = lax.scan(owner_pass, start, (tile_groups, token_groups, pooled_groups, live_tiles))
    tile_grad = grads.reshape(tiles.shape)
    return (tile_grad, totals[0], totals[1])
```

```python
import functools
import jax
import jax.numpy as jnp
from jax import lax
from jax.experimental import pallas as pl
from jax.experimental.pallas import tpu as pltpu
from jax.sharding import PartitionSpec as P

sqrt_two_pi = 0.7978845608028654
cubic_coef = 0.044715
LANES = 128
F32 = jnp.float32
BF16 = jnp.bfloat16
WHOLE = pl.BlockSpec(memory_space=pltpu.VMEM)
SCALARS = pl.BlockSpec(memory_space=pltpu.SMEM)
APART = pl.BlockSpec(memory_space=pl.ANY)


def depthwise_lanes(rows, taps_ref, lanes, reach, flip):
    height, width = len(rows), rows[0].shape[0]
    margin = reach // 2
    place = lax.broadcasted_iota(jnp.int32, rows[0].shape, 0)
    total = [None] * height
    for col in range(reach):
        shift = col - margin
        if shift:
            inside = (place + shift >= 0) & (place + shift < width)
            moved = [jnp.where(inside, pltpu.roll(row, (-shift) % width, 0), 0.0) for row in rows]
        else:
            moved = rows
        for line in range(reach):
            index = line * reach + col
            if flip:
                index = reach * reach - 1 - index
            tap = jnp.broadcast_to(taps_ref[pl.ds(index, 1), lanes], rows[0].shape)
            for u in range(height):
                source = u + line - margin
                if 0 <= source < height:
                    term = moved[source] * tap
                    total[u] = term if total[u] is None else total[u] + term
    return total


def front_kernel(reach, base_ref, tiles_ref, taps_ref, bias_ref, gain_ref, shift_ref, normed_ref, normal_ref, inv_ref, conv_ref):
    height, width = tiles_ref.shape[1:3]
    channels = tiles_ref.shape[3]

    def slab(block, carry):
        lanes = pl.ds(pl.multiple_of(block * LANES, LANES), LANES)
        rows = [tiles_ref[0, u, :, lanes].astype(F32) for u in range(height)]
        total = depthwise_lanes(rows, taps_ref, lanes, reach, False)
        for u in range(height):
            conv_ref[u * width : (u + 1) * width, lanes] = total[u] + bias_ref[:, lanes]
        return carry

    lax.fori_loop(0, channels // LANES, slab, 0)
    conv = conv_ref[...]
    center = jnp.mean(conv, axis=-1, keepdims=True)
    shifted = conv - center
    inv = lax.rsqrt(jnp.mean(shifted * shifted, axis=-1, keepdims=True) + 1e-06)
    normal = shifted * inv
    normal_ref[...] = normal
    inv_ref[...] = jnp.broadcast_to(inv, inv_ref.shape)
    normed_ref[...] = (normal * gain_ref[...] + shift_ref[...]).astype(BF16)


def front(base, tiles, taps, bias, gain, shift, mine, reach):
    _, height, width, channels = tiles.shape
    spots = height * width
    one = lambda i, b: (0, 0)
    return pl.pallas_call(
        functools.partial(front_kernel, reach),
        name="conv_norm",
        out_shape=(
            jax.ShapeDtypeStruct((mine * spots, channels), BF16),
            jax.ShapeDtypeStruct((mine * spots, channels), F32),
            jax.ShapeDtypeStruct((mine * spots, LANES), F32),
        ),
        grid_spec=pltpu.PrefetchScalarGridSpec(
            num_scalar_prefetch=1,
            grid=(mine,),
            in_specs=[
                pl.BlockSpec((1, height, width, channels), lambda i, b: (b[0] + i, 0, 0, 0)),
                pl.BlockSpec(taps.shape, one),
                pl.BlockSpec((1, channels), one),
                pl.BlockSpec((1, channels), one),
                pl.BlockSpec((1, channels), one),
            ],
            out_specs=[
                pl.BlockSpec((spots, channels), lambda i, b: (i, 0)),
                pl.BlockSpec((spots, channels), lambda i, b: (i, 0)),
                pl.BlockSpec((spots, LANES), lambda i, b: (i, 0)),
            ],
            scratch_shapes=[pltpu.VMEM((spots, channels), F32)],
        ),
    )(base, tiles, taps, bias, gain, shift)


def gather_rows(at_ref, pieces, whole_ref, sems):
    rows = pieces[0].shape[0]
    copies = [
        pltpu.make_async_copy(piece, whole_ref.at[pl.ds(pl.multiple_of(at_ref[k], 16), rows)], sems.at[k])
        for k, piece in enumerate(pieces)
    ]
    for copy in copies:
        copy.start()
    for copy in copies:
        copy.wait()


def across_rows(left, right):
    return lax.dot_general(left, right, (((0,), (0,)), ((), ())), preferred_element_type=F32)


ROWS = 32


def up_kernel(count, at_ref, own_n, other_n, own_b, other_b, bias_ref, *rest):
    pieces, (slope_ref, down_ref, weight_ref, hidden_ref, act_ref, sems) = rest[:count], rest[count:]
    gather_rows(at_ref, pieces, weight_ref, sems)
    rows = own_n.shape[0]
    for half, normed in enumerate((own_n, other_n)):
        hidden_ref[...] = jnp.dot(normed[...], weight_ref[...], preferred_element_type=F32)

        def block(i, carry):
            here = pl.ds(pl.multiple_of(i * ROWS, ROWS), ROWS)
            value = hidden_ref[here, :] + bias_ref[...]
            square = value * value
            tangent = jnp.tanh(value * (sqrt_two_pi + (sqrt_two_pi * cubic_coef) * square))
            upper = 0.5 + 0.5 * tangent
            act_ref[half, here, :] = (value * upper).astype(BF16)
            bend = (0.5 * value) * (1.0 - tangent * tangent)
            slope = upper + bend * (sqrt_two_pi + (3.0 * sqrt_two_pi * cubic_coef) * square)
            slope_ref[half, here, :] = slope
            return carry

        lax.fori_loop(0, rows // ROWS, block, 0)
    down_ref[...] = (across_rows(own_b[...], act_ref[0]) + across_rows(other_b[...], act_ref[1])).astype(BF16)


def up(at, own_n, other_n, own_b, other_b, bias, pieces):
    rows, channels = own_n.shape
    columns = pieces[0].shape[1]
    return pl.pallas_call(
        functools.partial(up_kernel, len(pieces)),
        name="up_and_down_grad",
        out_shape=(
            jax.ShapeDtypeStruct((2, rows, columns), F32),
            jax.ShapeDtypeStruct((channels, columns), BF16),
            jax.ShapeDtypeStruct((channels, columns), BF16),
        ),
        in_specs=[SCALARS] + [WHOLE] * 5 + [APART] * len(pieces),
        out_specs=[WHOLE] * 3,
        scratch_shapes=[
            pltpu.VMEM((rows, columns), F32),
            pltpu.VMEM((2, rows, columns), BF16),
            pltpu.SemaphoreType.DMA((len(pieces),)),
        ],
        compiler_params=pltpu.CompilerParams(vmem_limit_bytes=40 << 20),
    )(at, own_n, other_n, own_b, other_b, bias, *pieces)


def down_kernel(count, at_ref, own_n, other_n, own_b, other_b, slope_ref, *rest):
    pieces, (grad_ref, up_ref, weight_ref, acted_ref, sems) = rest[:count], rest[count:]
    gather_rows(at_ref, pieces, weight_ref, sems)
    rows = own_n.shape[0]
    for half, branch in enumerate((own_b, other_b)):
        acted_ref[...] = jnp.dot(branch[...], weight_ref[...], preferred_element_type=F32)

        def block(i, carry):
            here = pl.ds(pl.multiple_of(i * ROWS, ROWS), ROWS)
            grad_ref[half, here, :] = (acted_ref[here, :] * slope_ref[half, here, :]).astype(BF16)
            return carry

        lax.fori_loop(0, rows // ROWS, block, 0)
    up_ref[...] = (across_rows(own_n[...], grad_ref[0]) + across_rows(other_n[...], grad_ref[1])).astype(BF16)


def down(at, own_n, other_n, own_b, other_b, slope, pieces):
    rows, channels = own_n.shape
    columns = pieces[0].shape[1]
    return pl.pallas_call(
        functools.partial(down_kernel, len(pieces)),
        name="hidden_and_up_grad",
        out_shape=(
            jax.ShapeDtypeStruct((2, rows, columns), BF16),
            jax.ShapeDtypeStruct((channels, columns), BF16),
        ),
        in_specs=[SCALARS] + [WHOLE] * 5 + [APART] * len(pieces),
        out_specs=[WHOLE] * 2,
        scratch_shapes=[
            pltpu.VMEM((channels, columns), BF16),
            pltpu.VMEM((rows, columns), F32),
            pltpu.SemaphoreType.DMA((len(pieces),)),
        ],
        compiler_params=pltpu.CompilerParams(vmem_limit_bytes=40 << 20),
    )(at, own_n, other_n, own_b, other_b, slope, *pieces)


def back_kernel(core_ref, grad_ref, weight_ref, keep_ref, send_ref):
    rows = grad_ref.shape[1] // 2
    core = core_ref[0]
    for half in range(2):
        for target, side in ((keep_ref, core), (send_ref, 1 - core)):
            here = pl.ds(pl.multiple_of(side * rows, rows), rows)
            target[half] = lax.dot_general(
                grad_ref[half, here, :], weight_ref[...], (((1,), (1,)), ((), ())), preferred_element_type=F32
            ).astype(BF16)


def back(core, grad, weight):
    half = jax.ShapeDtypeStruct((2, grad.shape[1] // 2, weight.shape[0]), BF16)
    return pl.pallas_call(
        back_kernel,
        name="normed_grad",
        out_shape=(half, half),
        in_specs=[SCALARS, WHOLE, WHOLE],
        out_specs=[WHOLE] * 2,
        compiler_params=pltpu.CompilerParams(vmem_limit_bytes=40 << 20),
    )(core, grad, weight)


def tail_kernel(
    reach, base_ref, live_ref, near_ref, core_ref, far_ref, normal_ref, inv_ref, token_ref, pooled_ref, taps_ref, gain_ref, out_ref, conv_ref
):
    height, width, channels = token_ref.shape[1:]
    tile = base_ref[0] + pl.program_id(0)
    live = (tile < live_ref[0]).astype(F32)
    total = near_ref[0].astype(F32) + core_ref[0].astype(F32) + far_ref[...].astype(F32)
    scaled = total * gain_ref[...]
    normal = normal_ref[...]
    center = jnp.mean(scaled, axis=-1, keepdims=True)
    along = jnp.mean(scaled * normal, axis=-1, keepdims=True)
    conv_ref[...] = (scaled - center - normal * along) * inv_ref[:, :1]

    def slab(block, carry):
        lanes = pl.ds(pl.multiple_of(block * LANES, LANES), LANES)
        rows = [conv_ref[u * width : (u + 1) * width, lanes] for u in range(height)]
        total = depthwise_lanes(rows, taps_ref, lanes, reach, True)
        pooled = pooled_ref[0, :, lanes]
        for u in range(height):
            out_grad = live * token_ref[0, u, :, lanes].astype(F32) + pooled
            out_ref[0, u, :, lanes] = (out_grad + total[u]).astype(BF16)
        return carry

    lax.fori_loop(0, channels // LANES, slab, 0)


def tail(base, live, keep, core, far, normal, inv, token, pooled, taps, gain, reach):
    _, height, width, channels = token.shape
    spots = height * width
    mine = normal.shape[0] // spots
    one = lambda i, b, n: (0, 0)
    rows = lambda i, b, n: (i, 0)
    first = lambda i, b, n: (0, i, 0)
    return pl.pallas_call(
        functools.partial(tail_kernel, reach),
        name="norm_conv_back",
        out_shape=jax.ShapeDtypeStruct((mine, height, width, channels), BF16),
        grid_spec=pltpu.PrefetchScalarGridSpec(
            num_scalar_prefetch=2,
            grid=(mine,),
            in_specs=[
                pl.BlockSpec((1, spots, channels), first),
                pl.BlockSpec((1, spots, channels), first),
                pl.BlockSpec((spots, channels), rows),
                pl.BlockSpec((spots, channels), rows),
                pl.BlockSpec((spots, LANES), rows),
                pl.BlockSpec((1, height, width, channels), lambda i, b, n: (b[0] + i, 0, 0, 0)),
                pl.BlockSpec((1, 1, channels), lambda i, b, n: (b[0] + i, 0, 0)),
                pl.BlockSpec(taps.shape, one),
                pl.BlockSpec((1, channels), one),
            ],
            out_specs=pl.BlockSpec((1, height, width, channels), lambda i, b, n: (i, 0, 0, 0)),
            scratch_shapes=[pltpu.VMEM((spots, channels), F32)],
        ),
    )(base, live, keep, core, far, normal, inv, token, pooled[:, None, :], taps, gain)


def on_device(
    sizes,
    tiles,
    token_grad,
    embed_grad,
    live_tiles,
    dw_kernel,
    dw_bias,
    ln_gain,
    ln_bias,
    w_up,
    b_up,
    w_down,
    layer_scale,
):
    n_seq, n_dp = sizes
    count, height, width, channels = tiles.shape
    reach = dw_kernel.shape[0]
    mine = count // 2
    spots = height * width
    shard, columns = w_up.shape
    part = columns // 2
    seq, dp, core = lax.axis_index("seq"), lax.axis_index("dp"), lax.axis_index("mp")
    pair = [(i, i ^ 1) for i in range(n_dp)]
    ring = [(i, (i + 1) % n_seq) for i in range(n_seq)]
    side = (dp % 2) * part

    def over_ring(value):
        return lax.ppermute(value, "seq", ring)

    def over_pair(value):
        return lax.ppermute(value, "dp", pair)

    def over_cores(value):
        return lax.ppermute(value, "mp", [(0, 1), (1, 0)])

    def round_ring(weight):
        pieces = [lax.dynamic_slice_in_dim(weight, side, part, 1)]
        for _ in range(n_seq - 1):
            pieces.append(over_ring(pieces[-1]))
        return pieces

    def reduce_ring(partial):
        chunks = partial.reshape(n_seq, shard, part)

        def chunk(back):
            return lax.dynamic_index_in_dim(chunks, lax.rem(seq + (n_seq - back), n_seq), 0, keepdims=False)

        moving = chunk(1 % n_seq)
        for step in range(1, n_seq):
            moving = over_ring(moving).astype(F32) + chunk((step + 1) % n_seq).astype(F32)
            moving = moving.astype(BF16)
        return moving

    def both_sides(piece):
        if n_dp == 2:
            theirs = over_pair(piece)
            low = jnp.where(dp == 0, piece, theirs)
            high = jnp.where(dp == 0, theirs, piece)
            return jnp.concatenate([low, high], axis=1).astype(F32)
        spread = lax.dynamic_update_slice_in_dim(jnp.zeros((shard, columns), F32), piece.astype(F32), side, 1)
        return lax.psum(spread.astype(BF16), "dp").astype(F32)

    at = (lax.rem(seq + n_seq - jnp.arange(n_seq, dtype=jnp.int32), n_seq) * shard).astype(jnp.int32)
    base = (core * mine).astype(jnp.int32)[None]
    taps = dw_kernel.reshape(reach * reach, channels)
    row = lambda vector: vector.reshape(1, -1)

    up_pieces = round_ring(w_up)
    own_half, normal, inv = front(base, tiles, taps, row(dw_bias), row(ln_gain), row(ln_bias), mine, reach)
    other_half = over_pair(own_half)
    own_n = lax.all_gather(own_half, "mp", axis=0, tiled=True)
    arrived = lax.all_to_all(embed_grad[0], "seq", split_axis=0, concat_axis=1, tiled=True)
    live = (jnp.arange(count) < live_tiles[0]).astype(F32)
    pooled = arrived.astype(F32) * live[:, None] / spots
    out_grad = live[:, None, None, None] * token_grad.astype(F32) + pooled[:, None, None, :]
    own_b = (layer_scale * out_grad).astype(BF16).reshape(count * spots, channels)
    other_b = over_pair(lax.dynamic_slice_in_dim(own_b, core * (mine * spots), mine * spots, 0))
    down_pieces = round_ring(w_down)
    other_n = lax.all_gather(other_half, "mp", axis=0, tiled=True)
    other_b = lax.all_gather(other_b, "mp", axis=0, tiled=True)
    bias = row(lax.dynamic_slice_in_dim(b_up, side, part, 0))
    slope, part_down, whole_up = up(at, own_n, other_n, own_b, other_b, bias, up_pieces)
    down_sum = reduce_ring(part_down)
    hidden_grad, part_up = down(at, own_n, other_n, own_b, other_b, slope, down_pieces)
    up_sum = reduce_ring(part_up)
    keep, send = back(core.astype(jnp.int32)[None], hidden_grad, whole_up)
    from_core = over_cores(send)
    far = over_pair((keep[1].astype(F32) + from_core[1].astype(F32)).astype(BF16))
    grad_half = tail(base, live_tiles, keep, from_core, far, normal, inv, token_grad, pooled, taps, row(ln_gain), reach)
    tile_grad = lax.all_gather(grad_half, "mp", axis=0, tiled=True)
    return (tile_grad, both_sides(up_sum), both_sides(down_sum))


def solution(mesh):
    sizes = (mesh.shape["seq"], mesh.shape["dp"])
    return jax.shard_map(
        functools.partial(on_device, sizes),
        mesh=mesh,
        in_specs=(
            P(("groups", "seq", "dp"), None, None, None),
            P(("groups", "seq", "dp"), None, None, None),
            P("dp", "groups", "seq"),
            P(("groups", "seq", "dp")),
            P(),
            P(),
            P(),
            P(),
            P("seq", "mp"),
            P("mp"),
            P("seq", "mp"),
            P(),
        ),
        out_specs=(
            P(("groups", "seq", "dp"), None, None, None),
            P(("groups", "seq"), "mp"),
            P(("groups", "seq"), "mp"),
        ),
        check_vma=False,
    )
```

```python
import functools
import jax
import jax.numpy as jnp
from jax import lax
from jax.experimental import pallas as pl
from jax.experimental.pallas import tpu as pltpu
from jax.sharding import PartitionSpec as P

sqrt_two_pi = 0.7978845608028654
cubic_coef = 0.044715
LANES = 128
F32 = jnp.float32
BF16 = jnp.bfloat16
WHOLE = pl.BlockSpec(memory_space=pltpu.VMEM)
SCALARS = pl.BlockSpec(memory_space=pltpu.SMEM)
APART = pl.BlockSpec(memory_space=pltpu.HBM)


def in_vmem(*values):
    return [pltpu.with_memory_space_constraint(value, pltpu.VMEM) for value in values]


def in_hbm(*values):
    return [pltpu.with_memory_space_constraint(value, pltpu.HBM) for value in values]


ROWS = 32
VMEM_LIMIT = 16 << 20


COST = pl.CostEstimate(flops=10 << 30, transcendentals=0, bytes_accessed=4 << 20)


def depthwise_lanes(rows, taps_ref, lanes, reach, flip):
    height, width = len(rows), rows[0].shape[0]
    margin = reach // 2
    place = lax.broadcasted_iota(jnp.int32, rows[0].shape, 0)
    total = [None] * height
    for col in range(reach):
        shift = col - margin
        if shift:
            inside = (place + shift >= 0) & (place + shift < width)
            moved = [jnp.where(inside, pltpu.roll(row, (-shift) % width, 0), 0.0) for row in rows]
        else:
            moved = rows
        for line in range(reach):
            index = line * reach + col
            if flip:
                index = reach * reach - 1 - index
            tap = jnp.broadcast_to(taps_ref[index // reach, pl.ds(index % reach, 1), lanes], rows[0].shape)
            for u in range(height):
                source = u + line - margin
                if 0 <= source < height:
                    term = moved[source] * tap
                    total[u] = term if total[u] is None else total[u] + term
    return total


def front_kernel(
    base_ref, tiles_ref, taps_ref, bias_ref, gain_ref, shift_ref, normed_out, normal_out, inv_out,
    conv_ref, normed_ref, normal_ref, inv_ref, sems,
):
    height, width, channels = tiles_ref.shape[1:]
    spots = height * width
    mine = normed_ref.shape[0] // spots
    reach = taps_ref.shape[0]
    slabs = channels // LANES

    def saves(tile):
        here = pl.ds(pl.multiple_of(tile * spots, spots), spots)
        return (
            pltpu.make_async_copy(normal_ref.at[here], normal_out.at[here], sems.at[0, tile]),
            pltpu.make_async_copy(inv_ref.at[here], inv_out.at[here], sems.at[1, tile]),
            pltpu.make_async_copy(normed_ref.at[here], normed_out.at[here], sems.at[2, tile]),
        )

    def one_tile(tile, carry):
        def slab(block, carry):
            lanes = pl.ds(pl.multiple_of(block * LANES, LANES), LANES)
            rows = [tiles_ref[base_ref[0] + tile, u, :, lanes].astype(F32) for u in range(height)]
            total = depthwise_lanes(rows, taps_ref, lanes, reach, False)
            for u in range(height):
                conv_ref[u * width : (u + 1) * width, lanes] = total[u] + bias_ref[lanes][None, :]
            return carry

        lax.fori_loop(0, slabs, slab, 0)
        for part in range(spots // ROWS):
            conv = conv_ref[part * ROWS : (part + 1) * ROWS, :]
            here = pl.ds(pl.multiple_of(tile * spots + part * ROWS, ROWS), ROWS)
            center = jnp.mean(conv, axis=-1, keepdims=True)
            shifted = conv - center
            inv = lax.rsqrt(jnp.mean(shifted * shifted, axis=-1, keepdims=True) + 1e-06)
            normal = shifted * inv
            normal_ref[here, :] = normal
            inv_ref[here, :] = jnp.broadcast_to(inv, (ROWS, LANES))
            normed_ref[here, :] = (normal * gain_ref[...][None, :] + shift_ref[...][None, :]).astype(BF16)
        for copy in saves(tile):
            copy.start()
        return carry

    lax.fori_loop(0, mine, one_tile, 0)
    for tile in range(mine):
        for copy in saves(tile):
            copy.wait()


def front(base, tiles, taps, bias, gain, shift, mine):
    _, height, width, channels = tiles.shape
    rows = mine * height * width
    return pl.pallas_call(
        front_kernel,
        name="conv_norm",
        out_shape=(
            pltpu.HBM((rows, channels), BF16),
            pltpu.HBM((rows, channels), F32),
            pltpu.HBM((rows, LANES), F32),
        ),
        in_specs=[SCALARS] + [WHOLE] * 5,
        out_specs=[APART] * 3,
        scratch_shapes=[
            pltpu.VMEM((height * width, channels), F32),
            pltpu.VMEM((rows, channels), BF16),
            pltpu.VMEM((rows, channels), F32),
            pltpu.VMEM((rows, LANES), F32),
            pltpu.SemaphoreType.DMA((3, mine)),
        ],
        compiler_params=pltpu.CompilerParams(vmem_limit_bytes=VMEM_LIMIT),
        cost_estimate=COST,
    )(base, tiles, taps, bias, gain, shift)


def across_rows(left, right):
    return lax.dot_general(left, right, (((0,), (0,)), ((), ())), preferred_element_type=F32)


def up_kernel(hops, apart, place_ref, *rest):
    normed, branch, rest = rest[:4], rest[4:8], rest[8:]
    bias_ref, locals_, near, far = rest[0], rest[1:3], rest[3 : 3 + hops], rest[3 + hops : 3 + 2 * hops]
    slope_ref, down_ref, up_ref, fall_ref, normed_ref, branch_ref, hidden_ref, act_ref, sems = rest[3 + 2 * hops :]
    shard, half, part = locals_[0].shape[0], near[0].shape[1], up_ref.shape[1]
    rows = normed[0].shape[0]
    columns = pl.ds(pl.multiple_of(place_ref[0], LANES), part)
    early, late = [], []
    for which, whole_ref in enumerate((up_ref, fall_ref)):
        target = whole_ref.at[pl.ds(pl.multiple_of(place_ref[3], 16), shard)]
        moves = [(True, locals_[which].at[:, columns], target)]
        for k, (here, there) in enumerate(zip(near, far)):
            for is_far, piece, offset in ((0, here, place_ref[1]), (1, there, place_ref[2])):
                target = whole_ref.at[pl.ds(pl.multiple_of(place_ref[4 + k] + offset, 8), half)]
                moves.append((apart[2 * k + is_far], piece.at[which], target))
        for outside, source, target in moves:
            if outside:
                (late if which else early).append((source, target))
            else:
                target[...] = source[...]
    inputs = [(normed[k], normed_ref.at[k * rows : (k + 1) * rows]) for k in (0, 1)]
    copies = [pltpu.make_async_copy(source, target, sems.at[k]) for k, (source, target) in enumerate(early + inputs + late)]
    for copy in copies:
        copy.start()
    for k in (2, 3):
        normed_ref[k * rows : (k + 1) * rows, :] = normed[k][...]
    for k in range(4):
        branch_ref[k * rows : (k + 1) * rows, :] = branch[k][...]
    for copy in copies[: len(early)]:
        copy.wait()
    for k in (2, 3, 0, 1):
        if k < 2:
            copies[len(early) + k].wait()
        hidden_ref[...] = jnp.dot(normed_ref[k * rows : (k + 1) * rows, :], up_ref[...], preferred_element_type=F32)

        def block(i, carry):
            here = pl.ds(pl.multiple_of(i * ROWS, ROWS), ROWS)
            there = pl.ds(pl.multiple_of(k * rows + i * ROWS, ROWS), ROWS)
            value = hidden_ref[here, :] + bias_ref[...]
            square = value * value
            tangent = jnp.tanh(value * (sqrt_two_pi + (sqrt_two_pi * cubic_coef) * square))
            upper = 0.5 + 0.5 * tangent
            act_ref[there, :] = (value * upper).astype(BF16)
            bend = (0.5 * value) * (1.0 - tangent * tangent)
            slope_ref[there, :] = upper + bend * (sqrt_two_pi + (3.0 * sqrt_two_pi * cubic_coef) * square)
            return carry

        lax.fori_loop(0, rows // ROWS, block, 0)
    down_ref[...] = across_rows(branch_ref[...], act_ref[...]).astype(BF16)
    for copy in copies[len(early) + 2 :]:
        copy.wait()


def up(place, normed, branch, bias, weights, near, far):
    rows, channels = normed[0].shape
    columns = near[0].shape[2]
    hops = len(near)
    apart = [True] * (2 * hops)
    for last in (2 * hops - 1, 2 * hops - 2, 2 * hops - 3):
        apart[last] = False
    near = [(in_hbm if apart[2 * k] else in_vmem)(piece)[0] for k, piece in enumerate(near)]
    far = [(in_hbm if apart[2 * k + 1] else in_vmem)(piece)[0] for k, piece in enumerate(far)]
    pieces = [APART if apart[2 * k] else WHOLE for k in range(hops)] + [APART if apart[2 * k + 1] else WHOLE for k in range(hops)]
    return pl.pallas_call(
        functools.partial(up_kernel, hops, tuple(apart)),
        name="up_and_down_grad",
        out_shape=(
            pltpu.VMEM((4 * rows, columns), F32),
            pltpu.VMEM((channels, columns), BF16),
            pltpu.VMEM((channels, columns), BF16),
            pltpu.VMEM((channels, columns), BF16),
            pltpu.VMEM((4 * rows, channels), BF16),
            pltpu.VMEM((4 * rows, channels), BF16),
        ),
        in_specs=[SCALARS] + [APART] * 2 + [WHOLE] * 7 + [APART] * 2 + pieces,
        out_specs=[WHOLE] * 6,
        scratch_shapes=[
            pltpu.VMEM((rows, columns), F32),
            pltpu.VMEM((4 * rows, columns), BF16),
            pltpu.SemaphoreType.DMA((4 + 4 * hops,)),
        ],
        compiler_params=pltpu.CompilerParams(vmem_limit_bytes=VMEM_LIMIT),
        cost_estimate=COST,
    )(place, *in_hbm(*normed[:2]), *in_vmem(*normed[2:], *branch), bias, *in_hbm(*weights), *near, *far)


def down_kernel(branch_ref, slope_ref, weight_ref, grad_ref, acted_ref):
    rows = acted_ref.shape[0]
    for k in range(4):
        acted_ref[...] = jnp.dot(branch_ref[k * rows : (k + 1) * rows, :], weight_ref[...], preferred_element_type=F32)

        def block(i, carry):
            here = pl.ds(pl.multiple_of(i * ROWS, ROWS), ROWS)
            there = pl.ds(pl.multiple_of(k * rows + i * ROWS, ROWS), ROWS)
            grad_ref[there, :] = (acted_ref[here, :] * slope_ref[there, :]).astype(BF16)
            return carry

        lax.fori_loop(0, rows // ROWS, block, 0)


def down(branch, slope, weight):
    rows, columns = slope.shape
    return pl.pallas_call(
        down_kernel,
        name="hidden_grad",
        out_shape=pltpu.VMEM((rows, columns), BF16),
        in_specs=[WHOLE] * 3,
        out_specs=WHOLE,
        scratch_shapes=[pltpu.VMEM((rows // 4, columns), F32)],
        compiler_params=pltpu.CompilerParams(vmem_limit_bytes=VMEM_LIMIT),
        cost_estimate=COST,
    )(*in_vmem(branch, slope, weight))


def rise_kernel(normed_ref, grad_ref, up_ref):
    up_ref[...] = across_rows(normed_ref[...], grad_ref[...]).astype(BF16)


def rise(normed, grad):
    return pl.pallas_call(
        rise_kernel,
        name="up_grad",
        out_shape=pltpu.VMEM((normed.shape[1], grad.shape[1]), BF16),
        in_specs=[WHOLE] * 2,
        out_specs=WHOLE,
        compiler_params=pltpu.CompilerParams(vmem_limit_bytes=VMEM_LIMIT),
        cost_estimate=COST,
    )(*in_vmem(normed, grad))


def back_kernel(grad_ref, weight_ref, keep_ref, send_ref):
    rows = keep_ref.shape[1]
    for k, (target, slot) in enumerate(((keep_ref, 0), (send_ref, 0), (keep_ref, 1), (send_ref, 1))):
        target[slot] = lax.dot_general(
            grad_ref[k * rows : (k + 1) * rows, :], weight_ref[...], (((1,), (1,)), ((), ())), preferred_element_type=F32
        ).astype(BF16)


def back(grad, weight):
    rows, columns = grad.shape
    half = pltpu.VMEM((2, rows // 4, weight.shape[0]), BF16)
    return pl.pallas_call(
        back_kernel,
        name="normed_grad",
        out_shape=(half, half),
        in_specs=[WHOLE, WHOLE],
        out_specs=[WHOLE] * 2,
        compiler_params=pltpu.CompilerParams(vmem_limit_bytes=VMEM_LIMIT),
        cost_estimate=COST,
    )(*in_vmem(grad, weight))


def tail_kernel(
    base_ref, live_ref, normal_in, inv_in, token_in, near_ref, far_ref, taps_ref, pooled_ref, gain_ref, out_ref,
    normal_ref, inv_ref, token_ref, conv_ref, sems,
):
    mine, height, width, channels = out_ref.shape
    spots = height * width
    reach = taps_ref.shape[0]
    slabs = channels // LANES

    def loads(tile):
        here = pl.ds(pl.multiple_of(tile * spots, spots), spots)
        pairs = [(source.at[here], target.at[here]) for source, target in ((normal_in, normal_ref), (inv_in, inv_ref))]
        pairs.append((token_in.at[base_ref[0] + tile], token_ref.at[tile]))
        return [pltpu.make_async_copy(source, target, sems.at[k, tile]) for k, (source, target) in enumerate(pairs)]

    for tile in range(mine):
        for copy in loads(tile):
            copy.start()

    def one_tile(tile, carry):
        for copy in loads(tile):
            copy.wait()
        for part in range(spots // ROWS):
            here = pl.ds(pl.multiple_of(tile * spots + part * ROWS, ROWS), ROWS)
            scaled = (near_ref[here, :] + far_ref[here, :].astype(F32)) * gain_ref[...][None, :]
            normal = normal_ref[here, :]
            center = jnp.mean(scaled, axis=-1, keepdims=True)
            along = jnp.mean(scaled * normal, axis=-1, keepdims=True)
            conv_ref[part * ROWS : (part + 1) * ROWS, :] = (scaled - center - normal * along) * inv_ref[here, :1]
        live = (base_ref[0] + tile < live_ref[0]).astype(F32)

        def slab(block, carry):
            lanes = pl.ds(pl.multiple_of(block * LANES, LANES), LANES)
            rows = [conv_ref[u * width : (u + 1) * width, lanes] for u in range(height)]
            total = depthwise_lanes(rows, taps_ref, lanes, reach, True)
            pooled = pooled_ref[tile, :, lanes]
            for u in range(height):
                out_grad = live * token_ref[tile, u, :, lanes].astype(F32) + pooled
                out_ref[tile, u, :, lanes] = (out_grad + total[u]).astype(BF16)
            return carry

        lax.fori_loop(0, slabs, slab, 0)
        return carry

    lax.fori_loop(0, mine, one_tile, 0)


def tail(base, live, near, far, normal, inv, token, pooled, taps, gain):
    _, height, width, channels = token.shape
    rows = normal.shape[0]
    mine = rows // (height * width)
    return pl.pallas_call(
        tail_kernel,
        name="norm_conv_back",
        out_shape=jax.ShapeDtypeStruct((mine, height, width, channels), BF16),
        in_specs=[SCALARS] * 2 + [APART] * 3 + [WHOLE] * 5,
        out_specs=WHOLE,
        scratch_shapes=[
            pltpu.VMEM(normal.shape, F32),
            pltpu.VMEM(inv.shape, F32),
            pltpu.VMEM((mine, height, width, channels), BF16),
            pltpu.VMEM((height * width, channels), F32),
            pltpu.SemaphoreType.DMA((3, mine)),
        ],
        compiler_params=pltpu.CompilerParams(vmem_limit_bytes=VMEM_LIMIT),
        cost_estimate=COST,
    )(base, live, *in_hbm(normal, inv, token), *in_vmem(near, far), taps, pooled, gain)


def after(value, *others):
    return lax.optimization_barrier((value,) + others)[0]


def on_device(
    sizes,
    tiles,
    token_grad,
    embed_grad,
    live_tiles,
    dw_kernel,
    dw_bias,
    ln_gain,
    ln_bias,
    w_up,
    b_up,
    w_down,
    layer_scale,
):
    n_seq, n_dp = sizes
    count, height, width, channels = tiles.shape
    mine = count // 2
    spots = height * width
    shard, columns = w_up.shape
    part, half = columns // 2, shard // 2
    group, seq, dp, core = (lax.axis_index(name) for name in ("groups", "seq", "dp", "mp"))
    pair = [(i, i ^ 1) for i in range(n_dp)]
    swap = [(0, 1), (1, 0)]
    ring = [(i, (i + 1) % n_seq) for i in range(n_seq)]
    side = (dp % 2) * part

    def over_ring(value):
        return lax.ppermute(value, "seq", ring)

    def over_pair(value):
        return lax.ppermute(value, "dp", pair)

    def over_cores(value):
        return lax.ppermute(value, "mp", swap)

    def over_groups(value):
        return lax.ppermute(value, "groups", swap)

    def chunk(partial, back):
        chunks = partial.reshape(n_seq, shard, part)
        return lax.dynamic_index_in_dim(chunks, lax.rem(seq + (n_seq - back), n_seq), 0, keepdims=False)

    def hop(moving, partial, step):
        arrived = over_ring(moving).astype(F32) + chunk(partial, (step + 1) % n_seq).astype(F32)
        return arrived.astype(BF16)

    def both_sides(piece):
        if n_dp == 2:
            theirs = over_pair(piece)
            low = jnp.where(dp == 0, piece, theirs)
            high = jnp.where(dp == 0, theirs, piece)
            return jnp.concatenate([low, high], axis=1).astype(F32)
        spread = lax.dynamic_update_slice_in_dim(jnp.zeros((shard, columns), F32), piece.astype(F32), side, 1)
        return lax.psum(spread.astype(BF16), "dp").astype(F32)

    offsets = lax.rem(seq + n_seq - jnp.arange(n_seq, dtype=jnp.int32), n_seq) * shard
    place = jnp.concatenate([jnp.stack([side, group * half, (1 - group) * half]), offsets]).astype(jnp.int32)
    base = (core * mine).astype(jnp.int32)[None]

    moving = jnp.stack([lax.dynamic_slice(w, (group * half, side), (half, part)) for w in (w_up, w_down)])
    near, far = [over_ring(moving)], []
    live = (jnp.arange(count) < live_tiles[0]).astype(BF16)

    def own_tiles(values, which):
        return lax.dynamic_slice_in_dim(values, which * mine, mine, 0)

    own_token = own_tiles(token_grad, core) * own_tiles(live, core)[:, None, None, None]
    next_token = over_pair(own_token)
    base = after(base, moving, own_token)
    own_half, normal, inv = front(base, tiles, dw_kernel, dw_bias, ln_gain, ln_bias, mine)
    next_half = over_pair(own_half)
    core_half = over_cores(own_half)
    near[0] = after(near[0], own_half)
    for step in range(1, n_seq):
        far.append(over_groups(near[-1]))
        if step < n_seq - 1:
            near.append(after(over_ring(near[-1]), *far[: step - 1]))
    embed = lax.all_to_all(after(embed_grad[0], near[min(1, n_seq - 2)]), "seq", split_axis=0, concat_axis=1, tiled=True)
    pooled = after(embed, near[-1]) * live[:, None]
    next_pooled = over_pair(pooled)
    core_token = own_tiles(token_grad, 1 - core) * own_tiles(live, 1 - core)[:, None, None, None]

    def branch_grad(tokens, pools, which):
        own_pools = lax.dynamic_slice_in_dim(pools, which * mine, mine, 0).astype(F32) / spots
        return (layer_scale * (tokens.astype(F32) + own_pools[:, None, None, :])).astype(BF16).reshape(mine * spots, channels)

    branch = (
        branch_grad(own_token, pooled, core),
        branch_grad(core_token, pooled, 1 - core),
        branch_grad(next_token, next_pooled, core),
        branch_grad(over_cores(next_token), next_pooled, 1 - core),
    )
    bias = lax.dynamic_slice_in_dim(b_up, side, part, 0)[None, :]
    normed = (own_half, core_half, next_half, over_cores(next_half))
    slope, part_down, whole_up, whole_down, normed, branch = up(place, normed, branch, bias, (w_up, w_down), near, far)
    fall = hop(chunk(part_down, 1 % n_seq), part_down, 1)
    hidden_grad = down(branch, slope, whole_down)
    part_up = rise(normed, after(hidden_grad, fall))
    climb = chunk(part_up, 1 % n_seq)
    keep, send = back(after(hidden_grad, climb), whole_up)
    from_core = over_cores(send)
    from_pair = over_pair((keep[1].astype(F32) + from_core[1].astype(F32)).astype(BF16))
    near_grad = keep[0].astype(F32) + from_core[0].astype(F32)
    for step in range(1, n_seq):
        climb = hop(climb, part_up, step)
        if step < n_seq - 1:
            fall = hop(fall, part_down, step + 1)
        if step == 1:
            from_pair, climb, fall = lax.optimization_barrier((from_pair, climb, fall))
    own_pooled = lax.dynamic_slice_in_dim(pooled, core * mine, mine, 0).astype(F32)[:, None, :] / spots
    grad_half = tail(base, live_tiles, near_grad, from_pair, normal, inv, token_grad, own_pooled, dw_kernel, ln_gain)
    tile_grad = lax.all_gather(grad_half, "mp", axis=0, tiled=True)
    return (tile_grad, both_sides(climb), both_sides(fall))


def solution(mesh):
    sizes = (mesh.shape["seq"], mesh.shape["dp"])
    return jax.shard_map(
        functools.partial(on_device, sizes),
        mesh=mesh,
        in_specs=(
            P(("groups", "seq", "dp"), None, None, None),
            P(("groups", "seq", "dp"), None, None, None),
            P("dp", "groups", "seq"),
            P(("groups", "seq", "dp")),
            P(),
            P(),
            P(),
            P(),
            P("seq", "mp"),
            P("mp"),
            P("seq", "mp"),
            P(),
        ),
        out_specs=(
            P(("groups", "seq", "dp"), None, None, None),
            P(("groups", "seq"), "mp"),
            P(("groups", "seq"), "mp"),
        ),
        check_vma=False,
    )
```

```python
import functools
import jax
import jax.numpy as jnp
from jax import lax
from jax.experimental import pallas as pl
from jax.experimental.pallas import tpu as pltpu
from jax.sharding import PartitionSpec as P

sqrt_two_pi = 0.7978845608028654
cubic_coef = 0.044715
LANES = 128
F32 = jnp.float32
BF16 = jnp.bfloat16
WHOLE = pl.BlockSpec(memory_space=pltpu.VMEM)
SCALARS = pl.BlockSpec(memory_space=pltpu.SMEM)
APART = pl.BlockSpec(memory_space=pltpu.HBM)


def in_vmem(*values):
    return [pltpu.with_memory_space_constraint(value, pltpu.VMEM) for value in values]


def in_hbm(*values):
    return [pltpu.with_memory_space_constraint(value, pltpu.HBM) for value in values]


ROWS = 32
VMEM_LIMIT = 16 << 20


COST = pl.CostEstimate(flops=10 << 30, transcendentals=0, bytes_accessed=4 << 20)


def depthwise_lanes(rows, taps_ref, lanes, reach, flip):
    height, width = len(rows), rows[0].shape[0]
    margin = reach // 2
    place = lax.broadcasted_iota(jnp.int32, rows[0].shape, 0)
    total = [None] * height
    for col in range(reach):
        shift = col - margin
        if shift:
            inside = (place + shift >= 0) & (place + shift < width)
            moved = [jnp.where(inside, pltpu.roll(row, (-shift) % width, 0), 0.0) for row in rows]
        else:
            moved = rows
        for line in range(reach):
            index = line * reach + col
            if flip:
                index = reach * reach - 1 - index
            tap = jnp.broadcast_to(taps_ref[index // reach, pl.ds(index % reach, 1), lanes], rows[0].shape)
            for u in range(height):
                source = u + line - margin
                if 0 <= source < height:
                    term = moved[source] * tap
                    total[u] = term if total[u] is None else total[u] + term
    return total


def front_kernel(
    base_ref, tiles_ref, taps_ref, bias_ref, gain_ref, shift_ref, normed_out, normal_out, inv_out,
    conv_ref, normed_ref, normal_ref, inv_ref, sems,
):
    height, width, channels = tiles_ref.shape[1:]
    spots = height * width
    mine = normed_ref.shape[0] // spots
    reach = taps_ref.shape[0]
    slabs = channels // LANES

    def saves(tile):
        here = pl.ds(pl.multiple_of(tile * spots, spots), spots)
        return (
            pltpu.make_async_copy(normal_ref.at[here], normal_out.at[here], sems.at[0, tile]),
            pltpu.make_async_copy(inv_ref.at[here], inv_out.at[here], sems.at[1, tile]),
            pltpu.make_async_copy(normed_ref.at[here], normed_out.at[here], sems.at[2, tile]),
        )

    def one_tile(tile, carry):
        def slab(block, carry):
            lanes = pl.ds(pl.multiple_of(block * LANES, LANES), LANES)
            rows = [tiles_ref[base_ref[0] + tile, u, :, lanes].astype(F32) for u in range(height)]
            total = depthwise_lanes(rows, taps_ref, lanes, reach, False)
            for u in range(height):
                conv_ref[u * width : (u + 1) * width, lanes] = total[u] + bias_ref[lanes][None, :]
            return carry

        lax.fori_loop(0, slabs, slab, 0)
        for part in range(spots // ROWS):
            conv = conv_ref[part * ROWS : (part + 1) * ROWS, :]
            here = pl.ds(pl.multiple_of(tile * spots + part * ROWS, ROWS), ROWS)
            center = jnp.mean(conv, axis=-1, keepdims=True)
            shifted = conv - center
            inv = lax.rsqrt(jnp.mean(shifted * shifted, axis=-1, keepdims=True) + 1e-06)
            normal = shifted * inv
            normal_ref[here, :] = normal
            inv_ref[here, :] = jnp.broadcast_to(inv, (ROWS, LANES))
            normed_ref[here, :] = (normal * gain_ref[...][None, :] + shift_ref[...][None, :]).astype(BF16)
        for copy in saves(tile):
            copy.start()
        return carry

    lax.fori_loop(0, mine, one_tile, 0)
    for tile in range(mine):
        for copy in saves(tile):
            copy.wait()


def front(base, tiles, taps, bias, gain, shift, mine):
    _, height, width, channels = tiles.shape
    rows = mine * height * width
    return pl.pallas_call(
        front_kernel,
        name="conv_norm",
        out_shape=(
            pltpu.HBM((rows, channels), BF16),
            pltpu.HBM((rows, channels), F32),
            pltpu.HBM((rows, LANES), F32),
        ),
        in_specs=[SCALARS] + [WHOLE] * 5,
        out_specs=[APART] * 3,
        scratch_shapes=[
            pltpu.VMEM((height * width, channels), F32),
            pltpu.VMEM((rows, channels), BF16),
            pltpu.VMEM((rows, channels), F32),
            pltpu.VMEM((rows, LANES), F32),
            pltpu.SemaphoreType.DMA((3, mine)),
        ],
        compiler_params=pltpu.CompilerParams(vmem_limit_bytes=VMEM_LIMIT),
        cost_estimate=COST,
    )(base, tiles, taps, bias, gain, shift)


def store_chunks(seq, total, keep_ref, send_ref):
    shard = keep_ref.shape[1]
    count = total.shape[0] // shard

    def store(place):
        for chunk in range(count):
            away = chunk ^ place
            target = send_ref if away % 2 else keep_ref
            target[away // 2] = total[chunk * shard : (chunk + 1) * shard].astype(BF16)

    for place in range(count):
        pl.when(seq == place)(functools.partial(store, place))


def across_rows(left, right):
    return lax.dot_general(left, right, (((0,), (0,)), ((), ())), preferred_element_type=F32)


def lay_weight(place_ref, local, pieces, apart, whole_ref, sems):
    shard, part = local.shape[0], whole_ref.shape[1]
    pieces = [piece.at[:shard] for piece in pieces]
    columns = pl.ds(pl.multiple_of(place_ref[0], LANES), part)
    sources = [(True, local.at[:, columns])] + list(zip(apart, pieces))
    copies = []
    for k, (outside, source) in enumerate(sources):
        target = whole_ref.at[pl.ds(pl.multiple_of(place_ref[2 + k], 16), shard)]
        if outside:
            copies.append(pltpu.make_async_copy(source, target, sems.at[k]))
            copies[-1].start()
        else:
            target[...] = source[...]
    return copies


def activate(normed, weight_ref, bias_ref, hidden_ref, act_ref, slope_ref, first):
    hidden_ref[...] = jnp.dot(normed, weight_ref[...], preferred_element_type=F32)

    def block(i, carry):
        here = pl.ds(pl.multiple_of(i * ROWS, ROWS), ROWS)
        there = pl.ds(pl.multiple_of(first + i * ROWS, ROWS), ROWS)
        value = hidden_ref[here, :] + bias_ref[...]
        square = value * value
        tangent = jnp.tanh(value * (sqrt_two_pi + (sqrt_two_pi * cubic_coef) * square))
        upper = 0.5 + 0.5 * tangent
        act_ref[there, :] = (value * upper).astype(BF16)
        bend = (0.5 * value) * (1.0 - tangent * tangent)
        slope_ref[there, :] = upper + bend * (sqrt_two_pi + (3.0 * sqrt_two_pi * cubic_coef) * square)
        return carry

    lax.fori_loop(0, hidden_ref.shape[0] // ROWS, block, 0)


def up_kernel(apart, place_ref, own_ref, core_ref, bias_ref, local, *rest):
    hops = len(apart)
    pieces, (act_ref, slope_ref, up_ref, normed_ref, hidden_ref, sems) = rest[:hops], rest[hops:]
    rows = own_ref.shape[0]
    weights = lay_weight(place_ref, local, pieces, apart, up_ref, sems)
    inputs = [
        pltpu.make_async_copy(piece, normed_ref.at[k * rows : (k + 1) * rows], sems.at[1 + hops + k])
        for k, piece in enumerate((own_ref, core_ref))
    ]
    for copy in inputs:
        copy.start()
    for copy in weights:
        copy.wait()
    for k in range(2):
        inputs[k].wait()
        activate(normed_ref[k * rows : (k + 1) * rows, :], up_ref, bias_ref, hidden_ref, act_ref, slope_ref, k * rows)


def up_next_kernel(seq_ref, *rest):
    normed, branch, (bias_ref, up_ref, own_act_ref), rest = rest[:2], rest[2:6], rest[6:9], rest[9:]
    keep_ref, send_ref, slope_ref, normed_ref, branch_ref, hidden_ref, act_ref = rest
    rows = normed[0].shape[0]
    for k in range(2):
        activate(normed[k][...], up_ref, bias_ref, hidden_ref, act_ref, slope_ref, k * rows)
        normed_ref[k * rows : (k + 1) * rows, :] = normed[k][...]
    for k in range(4):
        branch_ref[k * rows : (k + 1) * rows, :] = branch[k][...]
    act = jnp.concatenate([own_act_ref[...], act_ref[...]], axis=0)
    store_chunks(seq_ref[0], across_rows(branch_ref[...], act), keep_ref, send_ref)


def sorted_pieces(pieces):
    apart = tuple(k < len(pieces) - 1 for k in range(len(pieces)))
    pieces = [(in_hbm if outside else in_vmem)(piece)[0] for outside, piece in zip(apart, pieces)]
    return apart, pieces, [APART if outside else WHOLE for outside in apart]


def up(place, own, core, bias, local, pieces):
    rows, channels = own.shape
    columns = pieces[0].shape[1]
    apart, pieces, specs = sorted_pieces(pieces)
    return pl.pallas_call(
        functools.partial(up_kernel, apart),
        name="hidden_own",
        out_shape=(
            pltpu.VMEM((2 * rows, columns), BF16),
            pltpu.VMEM((2 * rows, columns), F32),
            pltpu.VMEM((channels, columns), BF16),
            pltpu.VMEM((2 * rows, channels), BF16),
        ),
        in_specs=[SCALARS] + [APART] * 2 + [WHOLE] + [APART] + specs,
        out_specs=[WHOLE] * 4,
        scratch_shapes=[pltpu.VMEM((rows, columns), F32), pltpu.SemaphoreType.DMA((3 + len(pieces),))],
        compiler_params=pltpu.CompilerParams(vmem_limit_bytes=VMEM_LIMIT),
        cost_estimate=COST,
    )(place, *in_hbm(own, core), bias, *in_hbm(local), *pieces)


def up_next(seq, normed, branch, bias, weight, act, shard):
    rows, channels = normed[0].shape
    columns = weight.shape[1]
    chunks = pltpu.VMEM((channels // shard // 2, shard, columns), BF16)
    return pl.pallas_call(
        up_next_kernel,
        name="hidden_next_and_down_grad",
        out_shape=(
            chunks,
            chunks,
            pltpu.VMEM((2 * rows, columns), F32),
            pltpu.VMEM((2 * rows, channels), BF16),
            pltpu.VMEM((4 * rows, channels), BF16),
        ),
        in_specs=[SCALARS] + [WHOLE] * 9,
        out_specs=[WHOLE] * 5,
        scratch_shapes=[pltpu.VMEM((rows, columns), F32), pltpu.VMEM((2 * rows, columns), BF16)],
        compiler_params=pltpu.CompilerParams(vmem_limit_bytes=VMEM_LIMIT),
        cost_estimate=COST,
    )(seq, *in_vmem(*normed, *branch), bias, *in_vmem(weight, act))


def down_kernel(apart, place_ref, branch_ref, slope_own, slope_next, local, *rest):
    hops = len(apart)
    pieces, (grad_ref, weight_ref, acted_ref, sems) = rest[:hops], rest[hops:]
    for copy in lay_weight(place_ref, local, pieces, apart, weight_ref, sems):
        copy.wait()
    rows = acted_ref.shape[0]
    for k in range(4):
        acted_ref[...] = jnp.dot(branch_ref[k * rows : (k + 1) * rows, :], weight_ref[...], preferred_element_type=F32)

        def block(i, carry):
            here = pl.ds(pl.multiple_of(i * ROWS, ROWS), ROWS)
            there = pl.ds(pl.multiple_of(k * rows + i * ROWS, ROWS), ROWS)
            slope = pl.ds(pl.multiple_of(k % 2 * rows + i * ROWS, ROWS), ROWS)
            grad_ref[there, :] = (acted_ref[here, :] * (slope_next if k > 1 else slope_own)[slope, :]).astype(BF16)
            return carry

        lax.fori_loop(0, rows // ROWS, block, 0)


def down(place, branch, slopes, local, pieces):
    rows, columns = branch.shape[0], slopes[0].shape[1]
    apart, pieces, specs = sorted_pieces(pieces)
    return pl.pallas_call(
        functools.partial(down_kernel, apart),
        name="hidden_grad",
        out_shape=pltpu.VMEM((rows, columns), BF16),
        in_specs=[SCALARS] + [WHOLE] * 3 + [APART] + specs,
        out_specs=WHOLE,
        scratch_shapes=[
            pltpu.VMEM((branch.shape[1], columns), BF16),
            pltpu.VMEM((rows // 4, columns), F32),
            pltpu.SemaphoreType.DMA((1 + len(pieces),)),
        ],
        compiler_params=pltpu.CompilerParams(vmem_limit_bytes=VMEM_LIMIT),
        cost_estimate=COST,
    )(place, *in_vmem(branch, *slopes), *in_hbm(local), *pieces)


def rise_kernel(seq_ref, own_ref, next_ref, grad_ref, keep_ref, send_ref):
    normed = jnp.concatenate([own_ref[...], next_ref[...]], axis=0)
    store_chunks(seq_ref[0], across_rows(normed, grad_ref[...]), keep_ref, send_ref)


def rise(seq, normed, grad, shard):
    chunks = pltpu.VMEM((normed[0].shape[1] // shard // 2, shard, grad.shape[1]), BF16)
    return pl.pallas_call(
        rise_kernel,
        name="up_grad",
        out_shape=(chunks, chunks),
        in_specs=[SCALARS] + [WHOLE] * 3,
        out_specs=[WHOLE] * 2,
        compiler_params=pltpu.CompilerParams(vmem_limit_bytes=VMEM_LIMIT),
        cost_estimate=COST,
    )(seq, *in_vmem(*normed, grad))


def back_kernel(grad_ref, weight_ref, keep_ref, send_ref):
    rows = keep_ref.shape[1]
    for k, (target, slot) in enumerate(((keep_ref, 0), (send_ref, 0), (keep_ref, 1), (send_ref, 1))):
        target[slot] = lax.dot_general(
            grad_ref[k * rows : (k + 1) * rows, :], weight_ref[...], (((1,), (1,)), ((), ())), preferred_element_type=F32
        ).astype(BF16)


def back(grad, weight):
    rows, columns = grad.shape
    half = pltpu.VMEM((2, rows // 4, weight.shape[0]), BF16)
    return pl.pallas_call(
        back_kernel,
        name="normed_grad",
        out_shape=(half, half),
        in_specs=[WHOLE, WHOLE],
        out_specs=[WHOLE] * 2,
        compiler_params=pltpu.CompilerParams(vmem_limit_bytes=VMEM_LIMIT),
        cost_estimate=COST,
    )(*in_vmem(grad, weight))


def tail_kernel(
    base_ref, live_ref, normal_in, inv_in, token_in, taps_in, near_ref, far_ref, pooled_ref, gain_ref, out_ref,
    normal_ref, inv_ref, token_ref, taps_ref, conv_ref, sems, taps_sem,
):
    mine, height, width, channels = out_ref.shape
    spots = height * width
    reach = taps_ref.shape[0]
    slabs = channels // LANES

    def loads(tile):
        here = pl.ds(pl.multiple_of(tile * spots, spots), spots)
        pairs = [(source.at[here], target.at[here]) for source, target in ((normal_in, normal_ref), (inv_in, inv_ref))]
        pairs.append((token_in.at[base_ref[0] + tile], token_ref.at[tile]))
        return [pltpu.make_async_copy(source, target, sems.at[k, tile]) for k, (source, target) in enumerate(pairs)]

    load_taps = pltpu.make_async_copy(taps_in, taps_ref, taps_sem)
    load_taps.start()
    for tile in range(mine):
        for copy in loads(tile):
            copy.start()
    load_taps.wait()

    def one_tile(tile, carry):
        for copy in loads(tile):
            copy.wait()
        for part in range(spots // ROWS):
            here = pl.ds(pl.multiple_of(tile * spots + part * ROWS, ROWS), ROWS)
            scaled = (near_ref[here, :] + far_ref[here, :].astype(F32)) * gain_ref[...][None, :]
            normal = normal_ref[here, :]
            center = jnp.mean(scaled, axis=-1, keepdims=True)
            along = jnp.mean(scaled * normal, axis=-1, keepdims=True)
            conv_ref[part * ROWS : (part + 1) * ROWS, :] = (scaled - center - normal * along) * inv_ref[here, :1]
        live = (base_ref[0] + tile < live_ref[0]).astype(F32)

        def slab(block, carry):
            lanes = pl.ds(pl.multiple_of(block * LANES, LANES), LANES)
            rows = [conv_ref[u * width : (u + 1) * width, lanes] for u in range(height)]
            total = depthwise_lanes(rows, taps_ref, lanes, reach, True)
            pooled = pooled_ref[tile, :, lanes]
            for u in range(height):
                out_grad = live * token_ref[tile, u, :, lanes].astype(F32) + pooled
                out_ref[tile, u, :, lanes] = (out_grad + total[u]).astype(BF16)
            return carry

        lax.fori_loop(0, slabs, slab, 0)
        return carry

    lax.fori_loop(0, mine, one_tile, 0)


def tail(base, live, near, far, normal, inv, token, pooled, taps, gain):
    _, height, width, channels = token.shape
    rows = normal.shape[0]
    mine = rows // (height * width)
    return pl.pallas_call(
        tail_kernel,
        name="norm_conv_back",
        out_shape=jax.ShapeDtypeStruct((mine, height, width, channels), BF16),
        in_specs=[SCALARS] * 2 + [APART] * 4 + [WHOLE] * 4,
        out_specs=WHOLE,
        scratch_shapes=[
            pltpu.VMEM(normal.shape, F32),
            pltpu.VMEM(inv.shape, F32),
            pltpu.VMEM((mine, height, width, channels), BF16),
            pltpu.VMEM(taps.shape, F32),
            pltpu.VMEM((height * width, channels), F32),
            pltpu.SemaphoreType.DMA((3, mine)),
            pltpu.SemaphoreType.DMA,
        ],
        compiler_params=pltpu.CompilerParams(vmem_limit_bytes=VMEM_LIMIT),
        cost_estimate=COST,
    )(base, live, *in_hbm(normal, inv, token, taps), *in_vmem(near, far), pooled, gain)


def after(value, *others):
    return lax.optimization_barrier((value,) + others)[0]


def on_device(
    sizes,
    tiles,
    token_grad,
    embed_grad,
    live_tiles,
    dw_kernel,
    dw_bias,
    ln_gain,
    ln_bias,
    w_up,
    b_up,
    w_down,
    layer_scale,
):
    n_seq, n_dp = sizes
    count, height, width, channels = tiles.shape
    mine = count // 2
    spots = height * width
    shard, columns = w_up.shape
    part = columns // 2
    seq, dp, core = (lax.axis_index(name) for name in ("seq", "dp", "mp"))
    pair = [(i, i ^ 1) for i in range(n_dp)]
    swap = [(0, 1), (1, 0)]
    side = (dp % 2) * part

    def over_pair(value):
        return lax.ppermute(value, "dp", pair)

    def over_cores(value):
        return lax.ppermute(value, "mp", swap)

    def meet(value, step):
        return lax.ppermute(value, "seq", [(i, i ^ step) for i in range(n_seq)])

    def both_sides(piece, *others):
        if n_dp == 2:
            theirs = after(over_pair(piece), *others)
            low = jnp.where(dp == 0, piece, theirs)
            high = jnp.where(dp == 0, theirs, piece)
            return jnp.concatenate([low, high], axis=1).astype(F32)
        spread = lax.dynamic_update_slice_in_dim(jnp.zeros((shard, columns), F32), piece.astype(F32), side, 1)
        return lax.psum(spread.astype(BF16), "dp").astype(F32)

    offsets = (seq ^ jnp.arange(n_seq, dtype=jnp.int32)) * shard
    my_place = seq.astype(jnp.int32)[None]
    place = jnp.concatenate([jnp.stack([side, seq]), offsets]).astype(jnp.int32)
    base = (core * mine).astype(jnp.int32)[None]

    def own_tiles(values, which):
        return lax.dynamic_slice_in_dim(values, which * mine, mine, 0)

    live = (jnp.arange(count) < live_tiles[0]).astype(BF16)
    steps = [1 << level for level in range(n_seq.bit_length() - 1)]

    def spread(own, first):
        pieces = {0: own, **first}
        for r in range(1, n_seq):
            if r not in pieces:
                pieces[r] = meet(pieces[r ^ (r & -r)], r & -r)
        return [pieces[r] for r in range(1, n_seq)]

    embed = embed_grad[0]
    slots, width_ = embed.shape
    beside = part // width_
    deep = -(-slots // (16 * beside)) * 16
    embed = jnp.pad(embed, ((0, deep * beside - slots), (0, 0)))
    embed = jnp.concatenate([embed[k * deep : (k + 1) * deep] for k in range(beside)], axis=1)
    embed = jnp.pad(embed, ((0, 0), (0, part - beside * width_)))
    up_own = jnp.concatenate([lax.dynamic_slice_in_dim(w_up, side, part, 1), embed], axis=0)
    first = {r: meet(up_own, r) for r in steps}
    own_token = own_tiles(after(token_grad, up_own), core) * own_tiles(live, core)[:, None, None, None]
    next_token = over_pair(own_token)
    base = after(base, own_token)
    own_half, normal, inv = front(base, tiles, dw_kernel, dw_bias, ln_gain, ln_bias, mine)
    first, own_half = lax.optimization_barrier((first, own_half))
    up_pieces = spread(up_own, first)
    next_half = over_pair(own_half)
    core_half = over_cores(own_half)
    down_own = lax.dynamic_slice_in_dim(after(w_down, own_half), side, part, 1)
    first = {steps[-1]: meet(down_own, steps[-1])}
    up_pieces, core_half, next_token = lax.optimization_barrier((up_pieces, core_half, next_token))
    first = {**{r: meet(after(down_own, up_pieces), r) for r in steps[:-1]}, **first}
    parts = []
    for piece in [up_own] + up_pieces:
        packed = piece[shard:]
        packed = jnp.concatenate([packed[:, k * width_ : (k + 1) * width_] for k in range(beside)], axis=0)
        parts.append(lax.dynamic_slice_in_dim(packed, seq * count, count, 0))
    pooled = []
    for place_at in range(n_seq):
        block = parts[0]
        for r in range(1, n_seq):
            block = jnp.where(seq ^ place_at == r, parts[r], block)
        pooled.append(block)
    pooled = jnp.concatenate(pooled, axis=1) * live[:, None]
    next_pooled = over_pair(pooled)
    core_token = own_tiles(token_grad, 1 - core) * own_tiles(live, 1 - core)[:, None, None, None]

    def branch_grad(tokens, pools, which):
        own_pools = own_tiles(pools, which).astype(F32) / spots
        return (layer_scale * (tokens.astype(F32) + own_pools[:, None, None, :])).astype(BF16).reshape(mine * spots, channels)

    branch = (
        branch_grad(own_token, pooled, core),
        branch_grad(core_token, pooled, 1 - core),
        branch_grad(next_token, next_pooled, core),
        branch_grad(over_cores(next_token), next_pooled, 1 - core),
    )
    bias = lax.dynamic_slice_in_dim(b_up, side, part, 0)[None, :]
    act, slope, whole_up, normed = up(place, own_half, core_half, bias, w_up, up_pieces)
    down_pieces = spread(down_own, after(first, act, pooled))
    next_half = after(next_half, act)
    fall, fall_away, next_slope, next_normed, branch = up_next(
        my_place, (next_half, over_cores(next_half)), branch, bias, whole_up, act, shard
    )
    fall_from = meet(fall_away, 1)
    hidden_grad = down(place, branch, (slope, next_slope), w_down, down_pieces)

    def joined(keep, arrived):
        values = [keep[k].astype(F32) + arrived[k].astype(F32) for k in range(n_seq // 2)]
        return values[::2], [value.astype(BF16) for value in values[1::2]]

    def settle(values, away, *others):
        step = 2
        while away:
            arrived = after([meet(value, step) for value in away], *others)
            values = [value + more.astype(F32) for value, more in zip(values, arrived)]
            values, away = values[::2], [value.astype(BF16) for value in values[1::2]]
            step *= 2
        return values[0].astype(BF16)

    fall, fall_away = joined(fall, fall_from)
    climb, climb_away = rise(my_place, (normed, next_normed), hidden_grad, shard)
    climb_from = meet(climb_away, 1)
    keep, send = back(after(hidden_grad, climb, fall_away), whole_up)
    from_core = over_cores(send)
    far_grad = (keep[1].astype(F32) + from_core[1].astype(F32)).astype(BF16)
    from_pair = over_pair(far_grad)
    fall = settle(fall, fall_away, climb, from_pair)
    near_grad = after(keep[0].astype(F32) + from_core[0].astype(F32), fall)
    own_pooled = lax.dynamic_slice_in_dim(pooled, core * mine, mine, 0).astype(F32)[:, None, :] / spots
    grad_half = tail(base, live_tiles, near_grad, from_pair, normal, inv, token_grad, own_pooled, dw_kernel, ln_gain)
    climb, climb_away = joined(climb, after(climb_from, grad_half))
    climb = settle(climb, climb_away)
    other_half = over_cores(grad_half)
    first = jnp.where(core == 0, grad_half, other_half)
    second = jnp.where(core == 0, other_half, grad_half)
    tile_grad = jnp.concatenate([first, second], axis=0)
    grad_down = both_sides(fall)
    return (tile_grad, both_sides(climb, tile_grad, grad_down), grad_down)


def solution(mesh):
    sizes = (mesh.shape["seq"], mesh.shape["dp"])
    return jax.shard_map(
        functools.partial(on_device, sizes),
        mesh=mesh,
        in_specs=(
            P(("groups", "seq", "dp"), None, None, None),
            P(("groups", "seq", "dp"), None, None, None),
            P("dp", "groups", "seq"),
            P(("groups", "seq", "dp")),
            P(),
            P(),
            P(),
            P(),
            P("seq", "mp"),
            P("mp"),
            P("seq", "mp"),
            P(),
        ),
        out_specs=(
            P(("groups", "seq", "dp"), None, None, None),
            P(("groups", "seq"), "mp"),
            P(("groups", "seq"), "mp"),
        ),
        check_vma=False,
    )
```

```python
import functools
import jax
import jax.numpy as jnp
from jax import lax
from jax.experimental import pallas as pl
from jax.experimental.pallas import tpu as pltpu
from jax.sharding import PartitionSpec as P

sqrt_two_pi = 0.7978845608028654
cubic_coef = 0.044715
LANES = 128
F32 = jnp.float32
BF16 = jnp.bfloat16
WHOLE = pl.BlockSpec(memory_space=pltpu.VMEM)
SCALARS = pl.BlockSpec(memory_space=pltpu.SMEM)
APART = pl.BlockSpec(memory_space=pltpu.HBM)


def in_vmem(*values):
    return [pltpu.with_memory_space_constraint(value, pltpu.VMEM) for value in values]


def in_hbm(*values):
    return [pltpu.with_memory_space_constraint(value, pltpu.HBM) for value in values]


ROWS = 32
VMEM_LIMIT = 16 << 20


COST = pl.CostEstimate(flops=10 << 30, transcendentals=0, bytes_accessed=4 << 20)


def depthwise_lanes(rows, taps_ref, lanes, reach, flip):
    height, width = len(rows), rows[0].shape[0]
    margin = reach // 2
    place = lax.broadcasted_iota(jnp.int32, rows[0].shape, 0)
    total = [None] * height
    for col in range(reach):
        shift = col - margin
        if shift:
            inside = (place + shift >= 0) & (place + shift < width)
            moved = [jnp.where(inside, pltpu.roll(row, (-shift) % width, 0), 0.0) for row in rows]
        else:
            moved = rows
        for line in range(reach):
            index = line * reach + col
            if flip:
                index = reach * reach - 1 - index
            tap = jnp.broadcast_to(taps_ref[index // reach, pl.ds(index % reach, 1), lanes], rows[0].shape)
            for u in range(height):
                source = u + line - margin
                if 0 <= source < height:
                    term = moved[source] * tap
                    total[u] = term if total[u] is None else total[u] + term
    return total


def front_kernel(
    base_ref, tiles_ref, taps_ref, bias_ref, gain_ref, shift_ref, normed_out, normal_out, inv_out,
    conv_ref, normed_ref, normal_ref, inv_ref, sems,
):
    height, width, channels = tiles_ref.shape[1:]
    spots = height * width
    mine = normed_ref.shape[0] // spots
    reach = taps_ref.shape[0]
    slabs = channels // LANES

    def saves(tile):
        here = pl.ds(pl.multiple_of(tile * spots, spots), spots)
        return (
            pltpu.make_async_copy(normal_ref.at[here], normal_out.at[here], sems.at[0, tile]),
            pltpu.make_async_copy(inv_ref.at[here], inv_out.at[here], sems.at[1, tile]),
            pltpu.make_async_copy(normed_ref.at[here], normed_out.at[here], sems.at[2, tile]),
        )

    def one_tile(tile, carry):
        def slab(block, carry):
            lanes = pl.ds(pl.multiple_of(block * LANES, LANES), LANES)
            rows = [tiles_ref[base_ref[0] + tile, u, :, lanes].astype(F32) for u in range(height)]
            total = depthwise_lanes(rows, taps_ref, lanes, reach, False)
            for u in range(height):
                conv_ref[u * width : (u + 1) * width, lanes] = total[u] + bias_ref[lanes][None, :]
            return carry

        lax.fori_loop(0, slabs, slab, 0)
        for part in range(spots // ROWS):
            conv = conv_ref[part * ROWS : (part + 1) * ROWS, :]
            here = pl.ds(pl.multiple_of(tile * spots + part * ROWS, ROWS), ROWS)
            center = jnp.mean(conv, axis=-1, keepdims=True)
            shifted = conv - center
            inv = lax.rsqrt(jnp.mean(shifted * shifted, axis=-1, keepdims=True) + 1e-06)
            normal = shifted * inv
            normal_ref[here, :] = normal
            inv_ref[here, :] = jnp.broadcast_to(inv, (ROWS, LANES))
            normed_ref[here, :] = (normal * gain_ref[...][None, :] + shift_ref[...][None, :]).astype(BF16)
        for copy in saves(tile):
            copy.start()
        return carry

    lax.fori_loop(0, mine, one_tile, 0)
    for tile in range(mine):
        for copy in saves(tile):
            copy.wait()


def front(base, tiles, taps, bias, gain, shift, mine):
    _, height, width, channels = tiles.shape
    rows = mine * height * width
    return pl.pallas_call(
        front_kernel,
        name="conv_norm",
        out_shape=(
            pltpu.HBM((rows, channels), BF16),
            pltpu.HBM((rows, channels), F32),
            pltpu.HBM((rows, LANES), F32),
        ),
        in_specs=[SCALARS] + [WHOLE] * 5,
        out_specs=[APART] * 3,
        scratch_shapes=[
            pltpu.VMEM((height * width, channels), F32),
            pltpu.VMEM((rows, channels), BF16),
            pltpu.VMEM((rows, channels), F32),
            pltpu.VMEM((rows, LANES), F32),
            pltpu.SemaphoreType.DMA((3, mine)),
        ],
        compiler_params=pltpu.CompilerParams(vmem_limit_bytes=VMEM_LIMIT),
        cost_estimate=COST,
    )(base, tiles, taps, bias, gain, shift)


def store_chunks(seq, total, keep_ref, send_ref):
    shard = keep_ref.shape[1]
    count = total.shape[0] // shard

    def store(place):
        for chunk in range(count):
            away = chunk ^ place
            target = send_ref if away % 2 else keep_ref
            target[away // 2] = total[chunk * shard : (chunk + 1) * shard].astype(BF16)

    for place in range(count):
        pl.when(seq == place)(functools.partial(store, place))


def across_rows(left, right):
    return lax.dot_general(left, right, (((0,), (0,)), ((), ())), preferred_element_type=F32)


def lay_weight(place_ref, local, pieces, apart, whole_ref, sems):
    shard, part = local.shape[0], whole_ref.shape[1]
    pieces = [piece.at[:shard] for piece in pieces]
    columns = pl.ds(pl.multiple_of(place_ref[0], LANES), part)
    sources = [(True, local.at[:, columns])] + list(zip(apart, pieces))
    copies = []
    for k, (outside, source) in enumerate(sources):
        target = whole_ref.at[pl.ds(pl.multiple_of(place_ref[2 + k], 16), shard)]
        if outside:
            copies.append(pltpu.make_async_copy(source, target, sems.at[k]))
            copies[-1].start()
        else:
            target[...] = source[...]
    return copies


def activate(normed, weight_ref, bias_ref, hidden_ref, act_ref, slope_ref, first):
    hidden_ref[...] = jnp.dot(normed, weight_ref[...], preferred_element_type=F32)

    def block(i, carry):
        here = pl.ds(pl.multiple_of(i * ROWS, ROWS), ROWS)
        there = pl.ds(pl.multiple_of(first + i * ROWS, ROWS), ROWS)
        value = hidden_ref[here, :] + bias_ref[...]
        square = value * value
        tangent = jnp.tanh(value * (sqrt_two_pi + (sqrt_two_pi * cubic_coef) * square))
        upper = 0.5 + 0.5 * tangent
        act_ref[there, :] = (value * upper).astype(BF16)
        bend = (0.5 * value) * (1.0 - tangent * tangent)
        slope_ref[there, :] = upper + bend * (sqrt_two_pi + (3.0 * sqrt_two_pi * cubic_coef) * square)
        return carry

    lax.fori_loop(0, hidden_ref.shape[0] // ROWS, block, 0)


def up_kernel(apart, place_ref, own_ref, core_ref, bias_ref, local, *rest):
    hops = len(apart)
    pieces, (act_ref, slope_ref, up_ref, normed_ref, hidden_ref, sems) = rest[:hops], rest[hops:]
    rows = own_ref.shape[0]
    weights = lay_weight(place_ref, local, pieces, apart, up_ref, sems)
    inputs = [
        pltpu.make_async_copy(piece, normed_ref.at[k * rows : (k + 1) * rows], sems.at[1 + hops + k])
        for k, piece in enumerate((own_ref, core_ref))
    ]
    for copy in inputs:
        copy.start()
    for copy in weights:
        copy.wait()
    for k in range(2):
        inputs[k].wait()
        activate(normed_ref[k * rows : (k + 1) * rows, :], up_ref, bias_ref, hidden_ref, act_ref, slope_ref, k * rows)


def up_next_kernel(seq_ref, *rest):
    normed, branch, (bias_ref, up_ref, own_act_ref), rest = rest[:2], rest[2:6], rest[6:9], rest[9:]
    keep_ref, send_ref, slope_ref, normed_ref, branch_ref, hidden_ref, act_ref = rest
    rows = normed[0].shape[0]
    for k in range(2):
        activate(normed[k][...], up_ref, bias_ref, hidden_ref, act_ref, slope_ref, k * rows)
        normed_ref[k * rows : (k + 1) * rows, :] = normed[k][...]
    for k in range(4):
        branch_ref[k * rows : (k + 1) * rows, :] = branch[k][...]
    act = jnp.concatenate([own_act_ref[...], act_ref[...]], axis=0)
    store_chunks(seq_ref[0], across_rows(branch_ref[...], act), keep_ref, send_ref)


def sorted_pieces(pieces):
    apart = tuple(k < len(pieces) - 1 for k in range(len(pieces)))
    pieces = [(in_hbm if outside else in_vmem)(piece)[0] for outside, piece in zip(apart, pieces)]
    return apart, pieces, [APART if outside else WHOLE for outside in apart]


def up(place, own, core, bias, local, pieces):
    rows, channels = own.shape
    columns = pieces[0].shape[1]
    apart, pieces, specs = sorted_pieces(pieces)
    return pl.pallas_call(
        functools.partial(up_kernel, apart),
        name="hidden_own",
        out_shape=(
            pltpu.VMEM((2 * rows, columns), BF16),
            pltpu.VMEM((2 * rows, columns), F32),
            pltpu.VMEM((channels, columns), BF16),
            pltpu.VMEM((2 * rows, channels), BF16),
        ),
        in_specs=[SCALARS] + [APART] * 2 + [WHOLE] + [APART] + specs,
        out_specs=[WHOLE] * 4,
        scratch_shapes=[pltpu.VMEM((rows, columns), F32), pltpu.SemaphoreType.DMA((3 + len(pieces),))],
        compiler_params=pltpu.CompilerParams(vmem_limit_bytes=VMEM_LIMIT),
        cost_estimate=COST,
    )(place, *in_hbm(own, core), bias, *in_hbm(local), *pieces)


def up_next(seq, normed, branch, bias, weight, act, shard):
    rows, channels = normed[0].shape
    columns = weight.shape[1]
    chunks = pltpu.VMEM((channels // shard // 2, shard, columns), BF16)
    return pl.pallas_call(
        up_next_kernel,
        name="hidden_next_and_down_grad",
        out_shape=(
            chunks,
            chunks,
            pltpu.VMEM((2 * rows, columns), F32),
            pltpu.VMEM((2 * rows, channels), BF16),
            pltpu.VMEM((4 * rows, channels), BF16),
        ),
        in_specs=[SCALARS] + [WHOLE] * 9,
        out_specs=[WHOLE] * 5,
        scratch_shapes=[pltpu.VMEM((rows, columns), F32), pltpu.VMEM((2 * rows, columns), BF16)],
        compiler_params=pltpu.CompilerParams(vmem_limit_bytes=VMEM_LIMIT),
        cost_estimate=COST,
    )(seq, *in_vmem(*normed, *branch), bias, *in_vmem(weight, act))


def down_kernel(apart, place_ref, branch_ref, slope_own, slope_next, local, *rest):
    hops = len(apart)
    pieces, (grad_ref, weight_ref, acted_ref, sems) = rest[:hops], rest[hops:]
    for copy in lay_weight(place_ref, local, pieces, apart, weight_ref, sems):
        copy.wait()
    rows = acted_ref.shape[0]
    for k in range(4):
        acted_ref[...] = jnp.dot(branch_ref[k * rows : (k + 1) * rows, :], weight_ref[...], preferred_element_type=F32)

        def block(i, carry):
            here = pl.ds(pl.multiple_of(i * ROWS, ROWS), ROWS)
            there = pl.ds(pl.multiple_of(k * rows + i * ROWS, ROWS), ROWS)
            slope = pl.ds(pl.multiple_of(k % 2 * rows + i * ROWS, ROWS), ROWS)
            grad_ref[there, :] = (acted_ref[here, :] * (slope_next if k > 1 else slope_own)[slope, :]).astype(BF16)
            return carry

        lax.fori_loop(0, rows // ROWS, block, 0)


def down(place, branch, slopes, local, pieces):
    rows, columns = branch.shape[0], slopes[0].shape[1]
    apart, pieces, specs = sorted_pieces(pieces)
    return pl.pallas_call(
        functools.partial(down_kernel, apart),
        name="hidden_grad",
        out_shape=pltpu.VMEM((rows, columns), BF16),
        in_specs=[SCALARS] + [WHOLE] * 3 + [APART] + specs,
        out_specs=WHOLE,
        scratch_shapes=[
            pltpu.VMEM((branch.shape[1], columns), BF16),
            pltpu.VMEM((rows // 4, columns), F32),
            pltpu.SemaphoreType.DMA((1 + len(pieces),)),
        ],
        compiler_params=pltpu.CompilerParams(vmem_limit_bytes=VMEM_LIMIT),
        cost_estimate=COST,
    )(place, *in_vmem(branch, *slopes), *in_hbm(local), *pieces)


def rise_kernel(seq_ref, own_ref, next_ref, grad_ref, keep_ref, send_ref):
    normed = jnp.concatenate([own_ref[...], next_ref[...]], axis=0)
    store_chunks(seq_ref[0], across_rows(normed, grad_ref[...]), keep_ref, send_ref)


def rise(seq, normed, grad, shard):
    chunks = pltpu.VMEM((normed[0].shape[1] // shard // 2, shard, grad.shape[1]), BF16)
    return pl.pallas_call(
        rise_kernel,
        name="up_grad",
        out_shape=(chunks, chunks),
        in_specs=[SCALARS] + [WHOLE] * 3,
        out_specs=[WHOLE] * 2,
        compiler_params=pltpu.CompilerParams(vmem_limit_bytes=VMEM_LIMIT),
        cost_estimate=COST,
    )(seq, *in_vmem(*normed, grad))


def back_kernel(grad_ref, weight_ref, keep_ref, send_ref):
    rows = keep_ref.shape[1]
    for k, (target, slot) in enumerate(((keep_ref, 0), (send_ref, 0), (keep_ref, 1), (send_ref, 1))):
        target[slot] = lax.dot_general(
            grad_ref[k * rows : (k + 1) * rows, :], weight_ref[...], (((1,), (1,)), ((), ())), preferred_element_type=F32
        ).astype(BF16)


def back(grad, weight):
    rows, columns = grad.shape
    half = pltpu.VMEM((2, rows // 4, weight.shape[0]), BF16)
    return pl.pallas_call(
        back_kernel,
        name="normed_grad",
        out_shape=(half, half),
        in_specs=[WHOLE, WHOLE],
        out_specs=[WHOLE] * 2,
        compiler_params=pltpu.CompilerParams(vmem_limit_bytes=VMEM_LIMIT),
        cost_estimate=COST,
    )(*in_vmem(grad, weight))


def tail_kernel(
    base_ref, live_ref, normal_in, inv_in, token_in, taps_in, near_ref, far_ref, pooled_ref, gain_ref, out_ref,
    normal_ref, inv_ref, token_ref, taps_ref, conv_ref, sems, taps_sem,
):
    mine, height, width, channels = out_ref.shape
    spots = height * width
    reach = taps_ref.shape[0]
    slabs = channels // LANES

    def loads(tile):
        here = pl.ds(pl.multiple_of(tile * spots, spots), spots)
        pairs = [(source.at[here], target.at[here]) for source, target in ((normal_in, normal_ref), (inv_in, inv_ref))]
        pairs.append((token_in.at[base_ref[0] + tile], token_ref.at[tile]))
        return [pltpu.make_async_copy(source, target, sems.at[k, tile]) for k, (source, target) in enumerate(pairs)]

    load_taps = pltpu.make_async_copy(taps_in, taps_ref, taps_sem)
    load_taps.start()
    for tile in range(mine):
        for copy in loads(tile):
            copy.start()
    load_taps.wait()

    def one_tile(tile, carry):
        for copy in loads(tile):
            copy.wait()
        for part in range(spots // ROWS):
            here = pl.ds(pl.multiple_of(tile * spots + part * ROWS, ROWS), ROWS)
            scaled = (near_ref[here, :] + far_ref[here, :].astype(F32)) * gain_ref[...][None, :]
            normal = normal_ref[here, :]
            center = jnp.mean(scaled, axis=-1, keepdims=True)
            along = jnp.mean(scaled * normal, axis=-1, keepdims=True)
            conv_ref[part * ROWS : (part + 1) * ROWS, :] = (scaled - center - normal * along) * inv_ref[here, :1]
        live = (base_ref[0] + tile < live_ref[0]).astype(F32)

        def slab(block, carry):
            lanes = pl.ds(pl.multiple_of(block * LANES, LANES), LANES)
            rows = [conv_ref[u * width : (u + 1) * width, lanes] for u in range(height)]
            total = depthwise_lanes(rows, taps_ref, lanes, reach, True)
            pooled = pooled_ref[tile, :, lanes]
            for u in range(height):
                out_grad = live * token_ref[tile, u, :, lanes].astype(F32) + pooled
                out_ref[tile, u, :, lanes] = (out_grad + total[u]).astype(BF16)
            return carry

        lax.fori_loop(0, slabs, slab, 0)
        return carry

    lax.fori_loop(0, mine, one_tile, 0)


def tail(base, live, near, far, normal, inv, token, pooled, taps, gain):
    _, height, width, channels = token.shape
    rows = normal.shape[0]
    mine = rows // (height * width)
    return pl.pallas_call(
        tail_kernel,
        name="norm_conv_back",
        out_shape=jax.ShapeDtypeStruct((mine, height, width, channels), BF16),
        in_specs=[SCALARS] * 2 + [APART] * 4 + [WHOLE] * 4,
        out_specs=WHOLE,
        scratch_shapes=[
            pltpu.VMEM(normal.shape, F32),
            pltpu.VMEM(inv.shape, F32),
            pltpu.VMEM((mine, height, width, channels), BF16),
            pltpu.VMEM(taps.shape, F32),
            pltpu.VMEM((height * width, channels), F32),
            pltpu.SemaphoreType.DMA((3, mine)),
            pltpu.SemaphoreType.DMA,
        ],
        compiler_params=pltpu.CompilerParams(vmem_limit_bytes=VMEM_LIMIT),
        cost_estimate=COST,
    )(base, live, *in_hbm(normal, inv, token, taps), *in_vmem(near, far), pooled, gain)


def after(value, *others):
    return lax.optimization_barrier((value,) + others)[0]


def on_device(
    sizes,
    tiles,
    token_grad,
    embed_grad,
    live_tiles,
    dw_kernel,
    dw_bias,
    ln_gain,
    ln_bias,
    w_up,
    b_up,
    w_down,
    layer_scale,
):
    n_seq, n_dp = sizes
    count, height, width, channels = tiles.shape
    mine = count // 2
    spots = height * width
    shard, columns = w_up.shape
    part = columns // 2
    seq, dp, core = (lax.axis_index(name) for name in ("seq", "dp", "mp"))
    pair = [(i, i ^ 1) for i in range(n_dp)]
    swap = [(0, 1), (1, 0)]
    side = (dp % 2) * part

    def over_pair(value):
        return lax.ppermute(value, "dp", pair)

    def over_cores(value):
        return lax.ppermute(value, "mp", swap)

    def meet(value, step):
        return lax.ppermute(value, "seq", [(i, i ^ step) for i in range(n_seq)])

    def both_sides(piece, *others):
        if n_dp == 2:
            theirs = after(over_pair(piece), *others)
            low = jnp.where(dp == 0, piece, theirs)
            high = jnp.where(dp == 0, theirs, piece)
            return jnp.concatenate([low, high], axis=1).astype(F32)
        spread = lax.dynamic_update_slice_in_dim(jnp.zeros((shard, columns), F32), piece.astype(F32), side, 1)
        return lax.psum(spread.astype(BF16), "dp").astype(F32)

    offsets = (seq ^ jnp.arange(n_seq, dtype=jnp.int32)) * shard
    my_place = seq.astype(jnp.int32)[None]
    place = jnp.concatenate([jnp.stack([side, seq]), offsets]).astype(jnp.int32)
    base = (core * mine).astype(jnp.int32)[None]

    def own_tiles(values, which):
        return lax.dynamic_slice_in_dim(values, which * mine, mine, 0)

    live = (jnp.arange(count) < live_tiles[0]).astype(BF16)
    steps = [1 << level for level in range(n_seq.bit_length() - 1)]

    def spread(own, first):
        pieces = {0: own, **first}
        for r in range(1, n_seq):
            if r not in pieces:
                pieces[r] = meet(pieces[r ^ (r & -r)], r & -r)
        return [pieces[r] for r in range(1, n_seq)]

    embed = embed_grad[0]
    slots, width_ = embed.shape
    beside = part // width_
    deep = -(-slots // (16 * beside)) * 16
    embed = jnp.pad(embed, ((0, deep * beside - slots), (0, 0)))
    embed = jnp.concatenate([embed[k * deep : (k + 1) * deep] for k in range(beside)], axis=1)
    embed = jnp.pad(embed, ((0, 0), (0, part - beside * width_)))
    up_own = jnp.concatenate([lax.dynamic_slice_in_dim(w_up, side, part, 1), embed], axis=0)
    first = {r: meet(up_own, r) for r in steps}
    own_token = own_tiles(after(token_grad, up_own), core) * own_tiles(live, core)[:, None, None, None]
    next_token = over_pair(own_token)
    base = after(base, own_token)
    own_half, normal, inv = front(base, tiles, dw_kernel, dw_bias, ln_gain, ln_bias, mine)
    first, own_half = lax.optimization_barrier((first, own_half))
    up_pieces = spread(up_own, first)
    next_half = over_pair(own_half)
    core_half = over_cores(own_half)
    down_own = lax.dynamic_slice_in_dim(after(w_down, own_half), side, part, 1)
    first = {steps[-1]: meet(down_own, steps[-1])}
    up_pieces, core_half, next_token = lax.optimization_barrier((up_pieces, core_half, next_token))
    first = {**{r: meet(after(down_own, up_pieces), r) for r in steps[:-1]}, **first}
    parts = []
    for piece in [up_own] + up_pieces:
        packed = piece[shard:]
        packed = jnp.concatenate([packed[:, k * width_ : (k + 1) * width_] for k in range(beside)], axis=0)
        parts.append(lax.dynamic_slice_in_dim(packed, seq * count, count, 0))
    pooled = []
    for place_at in range(n_seq):
        block = parts[0]
        for r in range(1, n_seq):
            block = jnp.where(seq ^ place_at == r, parts[r], block)
        pooled.append(block)
    pooled = jnp.concatenate(pooled, axis=1) * live[:, None]
    next_pooled = over_pair(pooled)
    core_token = own_tiles(token_grad, 1 - core) * own_tiles(live, 1 - core)[:, None, None, None]

    def branch_grad(tokens, pools, which):
        own_pools = own_tiles(pools, which).astype(F32) / spots
        return (layer_scale * (tokens.astype(F32) + own_pools[:, None, None, :])).astype(BF16).reshape(mine * spots, channels)

    branch = (
        branch_grad(own_token, pooled, core),
        branch_grad(core_token, pooled, 1 - core),
        branch_grad(next_token, next_pooled, core),
        branch_grad(over_cores(next_token), next_pooled, 1 - core),
    )
    bias = lax.dynamic_slice_in_dim(b_up, side, part, 0)[None, :]
    act, slope, whole_up, normed = up(place, own_half, core_half, bias, w_up, up_pieces)
    down_pieces = spread(down_own, after(first, act, pooled))
    next_half = after(next_half, act)
    fall, fall_away, next_slope, next_normed, branch = up_next(
        my_place, (next_half, over_cores(next_half)), branch, bias, whole_up, act, shard
    )
    fall_from = meet(fall_away, 1)
    hidden_grad = down(place, branch, (slope, next_slope), w_down, down_pieces)

    def joined(keep, arrived):
        values = [keep[k].astype(F32) + arrived[k].astype(F32) for k in range(n_seq // 2)]
        return values[::2], [value.astype(BF16) for value in values[1::2]]

    def settle(values, away, *others):
        step = 2
        while away:
            arrived = after([meet(value, step) for value in away], *others)
            values = [value + more.astype(F32) for value, more in zip(values, arrived)]
            values, away = values[::2], [value.astype(BF16) for value in values[1::2]]
            step *= 2
        return values[0].astype(BF16)

    fall, fall_away = joined(fall, fall_from)
    climb, climb_away = rise(my_place, (normed, next_normed), hidden_grad, shard)
    climb_from = meet(climb_away, 1)
    climb, climb_away = joined(climb, climb_from)
    fall = settle(fall, fall_away)
    keep, send = back(after(hidden_grad, climb_away, fall), whole_up)
    from_core = over_cores(send)
    far_grad = (keep[1].astype(F32) + from_core[1].astype(F32)).astype(BF16)
    from_pair = over_pair(far_grad)
    climb = settle(climb, climb_away)
    near_grad = after(keep[0].astype(F32) + from_core[0].astype(F32), climb)
    own_pooled = lax.dynamic_slice_in_dim(pooled, core * mine, mine, 0).astype(F32)[:, None, :] / spots
    grad_half = tail(base, live_tiles, near_grad, from_pair, normal, inv, token_grad, own_pooled, dw_kernel, ln_gain)
    other_half = over_cores(grad_half)
    first = jnp.where(core == 0, grad_half, other_half)
    second = jnp.where(core == 0, other_half, grad_half)
    tile_grad = jnp.concatenate([first, second], axis=0)
    grad_down = both_sides(fall, grad_half)
    return (tile_grad, both_sides(climb, tile_grad, grad_down), grad_down)


def solution(mesh):
    sizes = (mesh.shape["seq"], mesh.shape["dp"])
    return jax.shard_map(
        functools.partial(on_device, sizes),
        mesh=mesh,
        in_specs=(
            P(("groups", "seq", "dp"), None, None, None),
            P(("groups", "seq", "dp"), None, None, None),
            P("dp", "groups", "seq"),
            P(("groups", "seq", "dp")),
            P(),
            P(),
            P(),
            P(),
            P("seq", "mp"),
            P("mp"),
            P("seq", "mp"),
            P(),
        ),
        out_specs=(
            P(("groups", "seq", "dp"), None, None, None),
            P(("groups", "seq"), "mp"),
            P(("groups", "seq"), "mp"),
        ),
        check_vma=False,
    )
```

```python
import functools
import jax
import jax.numpy as jnp
from jax import lax
from jax.experimental import pallas as pl
from jax.experimental.pallas import tpu as pltpu
from jax.sharding import PartitionSpec as P

sqrt_two_pi = 0.7978845608028654
cubic_coef = 0.044715
LANES = 128
F32 = jnp.float32
BF16 = jnp.bfloat16
WHOLE = pl.BlockSpec(memory_space=pltpu.VMEM)
SCALARS = pl.BlockSpec(memory_space=pltpu.SMEM)
APART = pl.BlockSpec(memory_space=pltpu.HBM)


def in_vmem(*values):
    return [pltpu.with_memory_space_constraint(value, pltpu.VMEM) for value in values]


def in_hbm(*values):
    return [pltpu.with_memory_space_constraint(value, pltpu.HBM) for value in values]


ROWS = 32
VMEM_LIMIT = 16 << 20


COST = pl.CostEstimate(flops=10 << 30, transcendentals=0, bytes_accessed=4 << 20)


def depthwise_lanes(rows, taps_ref, lanes, reach, flip):
    height, width = len(rows), rows[0].shape[0]
    margin = reach // 2
    place = lax.broadcasted_iota(jnp.int32, rows[0].shape, 0)
    total = [None] * height
    for col in range(reach):
        shift = col - margin
        if shift:
            inside = (place + shift >= 0) & (place + shift < width)
            moved = [jnp.where(inside, pltpu.roll(row, (-shift) % width, 0), 0.0) for row in rows]
        else:
            moved = rows
        for line in range(reach):
            index = line * reach + col
            if flip:
                index = reach * reach - 1 - index
            tap = jnp.broadcast_to(taps_ref[index // reach, pl.ds(index % reach, 1), lanes], rows[0].shape)
            for u in range(height):
                source = u + line - margin
                if 0 <= source < height:
                    term = moved[source] * tap
                    total[u] = term if total[u] is None else total[u] + term
    return total


def front_kernel(
    base_ref, tiles_ref, taps_ref, bias_ref, gain_ref, shift_ref, normed_out, normal_out, inv_out,
    conv_ref, normed_ref, normal_ref, inv_ref, sems,
):
    height, width, channels = tiles_ref.shape[1:]
    spots = height * width
    mine = normed_ref.shape[0] // spots
    reach = taps_ref.shape[0]
    slabs = channels // LANES

    def saves(tile):
        here = pl.ds(pl.multiple_of(tile * spots, spots), spots)
        return (
            pltpu.make_async_copy(normal_ref.at[here], normal_out.at[here], sems.at[0, tile]),
            pltpu.make_async_copy(inv_ref.at[here], inv_out.at[here], sems.at[1, tile]),
            pltpu.make_async_copy(normed_ref.at[here], normed_out.at[here], sems.at[2, tile]),
        )

    def one_tile(tile, carry):
        def slab(block, carry):
            lanes = pl.ds(pl.multiple_of(block * LANES, LANES), LANES)
            rows = [tiles_ref[base_ref[0] + tile, u, :, lanes].astype(F32) for u in range(height)]
            total = depthwise_lanes(rows, taps_ref, lanes, reach, False)
            for u in range(height):
                conv_ref[u * width : (u + 1) * width, lanes] = total[u] + bias_ref[lanes][None, :]
            return carry

        lax.fori_loop(0, slabs, slab, 0)
        for part in range(spots // ROWS):
            conv = conv_ref[part * ROWS : (part + 1) * ROWS, :]
            here = pl.ds(pl.multiple_of(tile * spots + part * ROWS, ROWS), ROWS)
            center = jnp.mean(conv, axis=-1, keepdims=True)
            shifted = conv - center
            inv = lax.rsqrt(jnp.mean(shifted * shifted, axis=-1, keepdims=True) + 1e-06)
            normal = shifted * inv
            normal_ref[here, :] = normal
            inv_ref[here, :] = jnp.broadcast_to(inv, (ROWS, LANES))
            normed_ref[here, :] = (normal * gain_ref[...][None, :] + shift_ref[...][None, :]).astype(BF16)
        for copy in saves(tile):
            copy.start()
        return carry

    lax.fori_loop(0, mine, one_tile, 0)
    for tile in range(mine):
        for copy in saves(tile):
            copy.wait()


def front(base, tiles, taps, bias, gain, shift, mine):
    _, height, width, channels = tiles.shape
    rows = mine * height * width
    return pl.pallas_call(
        front_kernel,
        name="conv_norm",
        out_shape=(
            pltpu.HBM((rows, channels), BF16),
            pltpu.HBM((rows, channels), F32),
            pltpu.HBM((rows, LANES), F32),
        ),
        in_specs=[SCALARS] + [WHOLE] * 5,
        out_specs=[APART] * 3,
        scratch_shapes=[
            pltpu.VMEM((height * width, channels), F32),
            pltpu.VMEM((rows, channels), BF16),
            pltpu.VMEM((rows, channels), F32),
            pltpu.VMEM((rows, LANES), F32),
            pltpu.SemaphoreType.DMA((3, mine)),
        ],
        compiler_params=pltpu.CompilerParams(vmem_limit_bytes=VMEM_LIMIT),
        cost_estimate=COST,
    )(base, tiles, taps, bias, gain, shift)


def store_chunks(seq, total, keep_ref, send_ref):
    shard = keep_ref.shape[1]
    count = total.shape[0] // shard

    def store(place):
        for chunk in range(count):
            away = chunk ^ place
            target = send_ref if away % 2 else keep_ref
            target[away // 2] = total[chunk * shard : (chunk + 1) * shard].astype(BF16)

    for place in range(count):
        pl.when(seq == place)(functools.partial(store, place))


def across_rows(left, right):
    return lax.dot_general(left, right, (((0,), (0,)), ((), ())), preferred_element_type=F32)


def lay_weight(place_ref, local, pieces, apart, whole_ref, sems):
    shard, part = local.shape[0], whole_ref.shape[1]
    pieces = [piece.at[:shard] for piece in pieces]
    columns = pl.ds(pl.multiple_of(place_ref[0], LANES), part)
    sources = [(True, local.at[:, columns])] + list(zip(apart, pieces))
    copies = []
    for k, (outside, source) in enumerate(sources):
        target = whole_ref.at[pl.ds(pl.multiple_of(place_ref[2 + k], 16), shard)]
        if outside:
            copies.append(pltpu.make_async_copy(source, target, sems.at[k]))
            copies[-1].start()
        else:
            target[...] = source[...]
    return copies


def activate(normed, weight_ref, bias_ref, hidden_ref, act_ref, slope_ref, first):
    hidden_ref[...] = jnp.dot(normed, weight_ref[...], preferred_element_type=F32)

    def block(i, carry):
        here = pl.ds(pl.multiple_of(i * ROWS, ROWS), ROWS)
        there = pl.ds(pl.multiple_of(first + i * ROWS, ROWS), ROWS)
        value = hidden_ref[here, :] + bias_ref[...]
        square = value * value
        tangent = jnp.tanh(value * (sqrt_two_pi + (sqrt_two_pi * cubic_coef) * square))
        upper = 0.5 + 0.5 * tangent
        act_ref[there, :] = (value * upper).astype(BF16)
        bend = (0.5 * value) * (1.0 - tangent * tangent)
        slope_ref[there, :] = upper + bend * (sqrt_two_pi + (3.0 * sqrt_two_pi * cubic_coef) * square)
        return carry

    lax.fori_loop(0, hidden_ref.shape[0] // ROWS, block, 0)


def up_kernel(apart, place_ref, own_ref, core_ref, bias_ref, local, *rest):
    hops = len(apart)
    pieces, (act_ref, slope_ref, up_ref, normed_ref, hidden_ref, sems) = rest[:hops], rest[hops:]
    rows = own_ref.shape[0]
    weights = lay_weight(place_ref, local, pieces, apart, up_ref, sems)
    inputs = [
        pltpu.make_async_copy(piece, normed_ref.at[k * rows : (k + 1) * rows], sems.at[1 + hops + k])
        for k, piece in enumerate((own_ref, core_ref))
    ]
    for copy in inputs:
        copy.start()
    for copy in weights:
        copy.wait()
    for k in range(2):
        inputs[k].wait()
        activate(normed_ref[k * rows : (k + 1) * rows, :], up_ref, bias_ref, hidden_ref, act_ref, slope_ref, k * rows)


def up_next_kernel(seq_ref, *rest):
    normed, branch, (bias_ref, up_ref, own_act_ref), rest = rest[:2], rest[2:6], rest[6:9], rest[9:]
    keep_ref, send_ref, slope_ref, normed_ref, branch_ref, hidden_ref, act_ref = rest
    rows = normed[0].shape[0]
    for k in range(2):
        activate(normed[k][...], up_ref, bias_ref, hidden_ref, act_ref, slope_ref, k * rows)
        normed_ref[k * rows : (k + 1) * rows, :] = normed[k][...]
    for k in range(4):
        branch_ref[k * rows : (k + 1) * rows, :] = branch[k][...]
    act = jnp.concatenate([own_act_ref[...], act_ref[...]], axis=0)
    store_chunks(seq_ref[0], across_rows(branch_ref[...], act), keep_ref, send_ref)


def sorted_pieces(pieces):
    apart = tuple(False for _ in pieces)
    pieces = [(in_hbm if outside else in_vmem)(piece)[0] for outside, piece in zip(apart, pieces)]
    return apart, pieces, [APART if outside else WHOLE for outside in apart]


def up(place, own, core, bias, local, pieces):
    rows, channels = own.shape
    columns = pieces[0].shape[1]
    apart, pieces, specs = sorted_pieces(pieces)
    return pl.pallas_call(
        functools.partial(up_kernel, apart),
        name="hidden_own",
        out_shape=(
            pltpu.VMEM((2 * rows, columns), BF16),
            pltpu.VMEM((2 * rows, columns), F32),
            pltpu.VMEM((channels, columns), BF16),
            pltpu.VMEM((2 * rows, channels), BF16),
        ),
        in_specs=[SCALARS] + [APART] * 2 + [WHOLE] + [APART] + specs,
        out_specs=[WHOLE] * 4,
        scratch_shapes=[pltpu.VMEM((rows, columns), F32), pltpu.SemaphoreType.DMA((3 + len(pieces),))],
        compiler_params=pltpu.CompilerParams(vmem_limit_bytes=VMEM_LIMIT),
        cost_estimate=COST,
    )(place, *in_hbm(own, core), bias, *in_hbm(local), *pieces)


def up_next(seq, normed, branch, bias, weight, act, shard):
    rows, channels = normed[0].shape
    columns = weight.shape[1]
    chunks = pltpu.VMEM((channels // shard // 2, shard, columns), BF16)
    return pl.pallas_call(
        up_next_kernel,
        name="hidden_next_and_down_grad",
        out_shape=(
            chunks,
            chunks,
            pltpu.VMEM((2 * rows, columns), F32),
            pltpu.VMEM((2 * rows, channels), BF16),
            pltpu.VMEM((4 * rows, channels), BF16),
        ),
        in_specs=[SCALARS] + [WHOLE] * 9,
        out_specs=[WHOLE] * 5,
        scratch_shapes=[pltpu.VMEM((rows, columns), F32), pltpu.VMEM((2 * rows, columns), BF16)],
        compiler_params=pltpu.CompilerParams(vmem_limit_bytes=VMEM_LIMIT),
        cost_estimate=COST,
    )(seq, *in_vmem(*normed, *branch), bias, *in_vmem(weight, act))


def down_kernel(apart, place_ref, branch_ref, slope_own, slope_next, local, *rest):
    hops = len(apart)
    pieces, (grad_ref, weight_ref, acted_ref, sems) = rest[:hops], rest[hops:]
    for copy in lay_weight(place_ref, local, pieces, apart, weight_ref, sems):
        copy.wait()
    rows = acted_ref.shape[0]
    for k in range(4):
        acted_ref[...] = jnp.dot(branch_ref[k * rows : (k + 1) * rows, :], weight_ref[...], preferred_element_type=F32)

        def block(i, carry):
            here = pl.ds(pl.multiple_of(i * ROWS, ROWS), ROWS)
            there = pl.ds(pl.multiple_of(k * rows + i * ROWS, ROWS), ROWS)
            slope = pl.ds(pl.multiple_of(k % 2 * rows + i * ROWS, ROWS), ROWS)
            grad_ref[there, :] = (acted_ref[here, :] * (slope_next if k > 1 else slope_own)[slope, :]).astype(BF16)
            return carry

        lax.fori_loop(0, rows // ROWS, block, 0)


def down(place, branch, slopes, local, pieces):
    rows, columns = branch.shape[0], slopes[0].shape[1]
    apart, pieces, specs = sorted_pieces(pieces)
    return pl.pallas_call(
        functools.partial(down_kernel, apart),
        name="hidden_grad",
        out_shape=pltpu.VMEM((rows, columns), BF16),
        in_specs=[SCALARS] + [WHOLE] * 3 + [APART] + specs,
        out_specs=WHOLE,
        scratch_shapes=[
            pltpu.VMEM((branch.shape[1], columns), BF16),
            pltpu.VMEM((rows // 4, columns), F32),
            pltpu.SemaphoreType.DMA((1 + len(pieces),)),
        ],
        compiler_params=pltpu.CompilerParams(vmem_limit_bytes=VMEM_LIMIT),
        cost_estimate=COST,
    )(place, *in_vmem(branch, *slopes), *in_hbm(local), *pieces)


def rise_kernel(seq_ref, own_ref, next_ref, grad_ref, keep_ref, send_ref):
    normed = jnp.concatenate([own_ref[...], next_ref[...]], axis=0)
    store_chunks(seq_ref[0], across_rows(normed, grad_ref[...]), keep_ref, send_ref)


def rise(seq, normed, grad, shard):
    chunks = pltpu.VMEM((normed[0].shape[1] // shard // 2, shard, grad.shape[1]), BF16)
    return pl.pallas_call(
        rise_kernel,
        name="up_grad",
        out_shape=(chunks, chunks),
        in_specs=[SCALARS] + [WHOLE] * 3,
        out_specs=[WHOLE] * 2,
        compiler_params=pltpu.CompilerParams(vmem_limit_bytes=VMEM_LIMIT),
        cost_estimate=COST,
    )(seq, *in_vmem(*normed, grad))


def back_kernel(grad_ref, weight_ref, keep_ref, send_ref):
    rows = keep_ref.shape[1]
    for k, (target, slot) in enumerate(((keep_ref, 0), (send_ref, 0), (keep_ref, 1), (send_ref, 1))):
        target[slot] = lax.dot_general(
            grad_ref[k * rows : (k + 1) * rows, :], weight_ref[...], (((1,), (1,)), ((), ())), preferred_element_type=F32
        ).astype(BF16)


def back(grad, weight):
    rows, columns = grad.shape
    half = pltpu.VMEM((2, rows // 4, weight.shape[0]), BF16)
    return pl.pallas_call(
        back_kernel,
        name="normed_grad",
        out_shape=(half, half),
        in_specs=[WHOLE, WHOLE],
        out_specs=[WHOLE] * 2,
        compiler_params=pltpu.CompilerParams(vmem_limit_bytes=VMEM_LIMIT),
        cost_estimate=COST,
    )(*in_vmem(grad, weight))


def tail_kernel(
    base_ref, live_ref, normal_in, inv_in, token_in, taps_in, near_ref, far_ref, pooled_ref, gain_ref, out_ref,
    normal_ref, inv_ref, token_ref, taps_ref, conv_ref, sems, taps_sem,
):
    mine, height, width, channels = out_ref.shape
    spots = height * width
    reach = taps_ref.shape[0]
    slabs = channels // LANES

    def loads(tile):
        here = pl.ds(pl.multiple_of(tile * spots, spots), spots)
        pairs = [(source.at[here], target.at[here]) for source, target in ((normal_in, normal_ref), (inv_in, inv_ref))]
        pairs.append((token_in.at[base_ref[0] + tile], token_ref.at[tile]))
        return [pltpu.make_async_copy(source, target, sems.at[k, tile]) for k, (source, target) in enumerate(pairs)]

    load_taps = pltpu.make_async_copy(taps_in, taps_ref, taps_sem)
    load_taps.start()
    for tile in range(mine):
        for copy in loads(tile):
            copy.start()
    load_taps.wait()

    def one_tile(tile, carry):
        for copy in loads(tile):
            copy.wait()
        for part in range(spots // ROWS):
            here = pl.ds(pl.multiple_of(tile * spots + part * ROWS, ROWS), ROWS)
            scaled = (near_ref[here, :] + far_ref[here, :].astype(F32)) * gain_ref[...][None, :]
            normal = normal_ref[here, :]
            center = jnp.mean(scaled, axis=-1, keepdims=True)
            along = jnp.mean(scaled * normal, axis=-1, keepdims=True)
            conv_ref[part * ROWS : (part + 1) * ROWS, :] = (scaled - center - normal * along) * inv_ref[here, :1]
        live = (base_ref[0] + tile < live_ref[0]).astype(F32)

        def slab(block, carry):
            lanes = pl.ds(pl.multiple_of(block * LANES, LANES), LANES)
            rows = [conv_ref[u * width : (u + 1) * width, lanes] for u in range(height)]
            total = depthwise_lanes(rows, taps_ref, lanes, reach, True)
            pooled = pooled_ref[tile, :, lanes]
            for u in range(height):
                out_grad = live * token_ref[tile, u, :, lanes].astype(F32) + pooled
                out_ref[tile, u, :, lanes] = (out_grad + total[u]).astype(BF16)
            return carry

        lax.fori_loop(0, slabs, slab, 0)
        return carry

    lax.fori_loop(0, mine, one_tile, 0)


def tail(base, live, near, far, normal, inv, token, pooled, taps, gain):
    _, height, width, channels = token.shape
    rows = normal.shape[0]
    mine = rows // (height * width)
    return pl.pallas_call(
        tail_kernel,
        name="norm_conv_back",
        out_shape=jax.ShapeDtypeStruct((mine, height, width, channels), BF16),
        in_specs=[SCALARS] * 2 + [APART] * 4 + [WHOLE] * 4,
        out_specs=WHOLE,
        scratch_shapes=[
            pltpu.VMEM(normal.shape, F32),
            pltpu.VMEM(inv.shape, F32),
            pltpu.VMEM((mine, height, width, channels), BF16),
            pltpu.VMEM(taps.shape, F32),
            pltpu.VMEM((height * width, channels), F32),
            pltpu.SemaphoreType.DMA((3, mine)),
            pltpu.SemaphoreType.DMA,
        ],
        compiler_params=pltpu.CompilerParams(vmem_limit_bytes=VMEM_LIMIT),
        cost_estimate=COST,
    )(base, live, *in_hbm(normal, inv, token, taps), *in_vmem(near, far), pooled, gain)


def after(value, *others):
    return lax.optimization_barrier((value,) + others)[0]


def on_device(
    sizes,
    tiles,
    token_grad,
    embed_grad,
    live_tiles,
    dw_kernel,
    dw_bias,
    ln_gain,
    ln_bias,
    w_up,
    b_up,
    w_down,
    layer_scale,
):
    n_seq, n_dp = sizes
    count, height, width, channels = tiles.shape
    mine = count // 2
    spots = height * width
    shard, columns = w_up.shape
    part = columns // 2
    seq, dp, core = (lax.axis_index(name) for name in ("seq", "dp", "mp"))
    pair = [(i, i ^ 1) for i in range(n_dp)]
    swap = [(0, 1), (1, 0)]
    side = (dp % 2) * part

    def over_pair(value):
        return lax.ppermute(value, "dp", pair)

    def over_cores(value):
        return lax.ppermute(value, "mp", swap)

    def meet(value, step):
        return lax.ppermute(value, "seq", [(i, i ^ step) for i in range(n_seq)])

    def both_sides(piece, *others):
        if n_dp == 2:
            theirs = after(over_pair(piece), *others)
            low = jnp.where(dp == 0, piece, theirs)
            high = jnp.where(dp == 0, theirs, piece)
            return jnp.concatenate([low, high], axis=1).astype(F32)
        spread = lax.dynamic_update_slice_in_dim(jnp.zeros((shard, columns), F32), piece.astype(F32), side, 1)
        return lax.psum(spread.astype(BF16), "dp").astype(F32)

    offsets = (seq ^ jnp.arange(n_seq, dtype=jnp.int32)) * shard
    my_place = seq.astype(jnp.int32)[None]
    place = jnp.concatenate([jnp.stack([side, seq]), offsets]).astype(jnp.int32)
    base = (core * mine).astype(jnp.int32)[None]

    def own_tiles(values, which):
        return lax.dynamic_slice_in_dim(values, which * mine, mine, 0)

    live = (jnp.arange(count) < live_tiles[0]).astype(BF16)
    steps = [1 << level for level in range(n_seq.bit_length() - 1)]

    def spread(own, first):
        pieces = {0: own, **first}
        for r in range(1, n_seq):
            if r not in pieces:
                pieces[r] = meet(pieces[r ^ (r & -r)], r & -r)
        return [pieces[r] for r in range(1, n_seq)]

    embed = embed_grad[0]
    slots, width_ = embed.shape
    beside = part // width_
    deep = -(-slots // (16 * beside)) * 16
    embed = jnp.pad(embed, ((0, deep * beside - slots), (0, 0)))
    embed = jnp.concatenate([embed[k * deep : (k + 1) * deep] for k in range(beside)], axis=1)
    embed = jnp.pad(embed, ((0, 0), (0, part - beside * width_)))
    up_own = jnp.concatenate([lax.dynamic_slice_in_dim(w_up, side, part, 1), embed], axis=0)
    first = {r: meet(up_own, r) for r in steps}
    own_token = own_tiles(after(token_grad, up_own), core) * own_tiles(live, core)[:, None, None, None]
    next_token = over_pair(own_token)
    base = after(base, own_token)
    own_half, normal, inv = front(base, tiles, dw_kernel, dw_bias, ln_gain, ln_bias, mine)
    first, own_half = lax.optimization_barrier((first, own_half))
    up_pieces = spread(up_own, first)
    next_half = over_pair(own_half)
    core_half = over_cores(own_half)
    down_own = lax.dynamic_slice_in_dim(after(w_down, own_half), side, part, 1)
    first = {steps[-1]: meet(down_own, steps[-1])}
    up_pieces, core_half, next_token = lax.optimization_barrier((up_pieces, core_half, next_token))
    first = {**{r: meet(after(down_own, up_pieces), r) for r in steps[:-1]}, **first}
    parts = []
    for piece in [up_own] + up_pieces:
        packed = piece[shard:]
        packed = jnp.concatenate([packed[:, k * width_ : (k + 1) * width_] for k in range(beside)], axis=0)
        parts.append(lax.dynamic_slice_in_dim(packed, seq * count, count, 0))
    pooled = []
    for place_at in range(n_seq):
        block = parts[0]
        for r in range(1, n_seq):
            block = jnp.where(seq ^ place_at == r, parts[r], block)
        pooled.append(block)
    pooled = jnp.concatenate(pooled, axis=1) * live[:, None]
    next_pooled = over_pair(pooled)
    core_token = own_tiles(token_grad, 1 - core) * own_tiles(live, 1 - core)[:, None, None, None]

    def branch_grad(tokens, pools, which):
        own_pools = own_tiles(pools, which).astype(F32) / spots
        return (layer_scale * (tokens.astype(F32) + own_pools[:, None, None, :])).astype(BF16).reshape(mine * spots, channels)

    branch = (
        branch_grad(own_token, pooled, core),
        branch_grad(core_token, pooled, 1 - core),
        branch_grad(next_token, next_pooled, core),
        branch_grad(over_cores(next_token), next_pooled, 1 - core),
    )
    bias = lax.dynamic_slice_in_dim(b_up, side, part, 0)[None, :]
    act, slope, whole_up, normed = up(place, own_half, core_half, bias, w_up, up_pieces)
    down_pieces = spread(down_own, after(first, act, pooled))
    next_half = after(next_half, act)
    fall, fall_away, next_slope, next_normed, branch = up_next(
        my_place, (next_half, over_cores(next_half)), branch, bias, whole_up, act, shard
    )
    fall_from = meet(fall_away, 1)
    hidden_grad = down(place, branch, (slope, next_slope), w_down, down_pieces)

    def joined(keep, arrived):
        values = [keep[k].astype(F32) + arrived[k].astype(F32) for k in range(n_seq // 2)]
        return values[::2], [value.astype(BF16) for value in values[1::2]]

    def settle(values, away, *others):
        step = 2
        while away:
            arrived = after([meet(value, step) for value in away], *others)
            values = [value + more.astype(F32) for value, more in zip(values, arrived)]
            values, away = values[::2], [value.astype(BF16) for value in values[1::2]]
            step *= 2
        return values[0].astype(BF16)

    fall, fall_away = joined(fall, fall_from)
    climb, climb_away = rise(my_place, (normed, next_normed), hidden_grad, shard)
    climb_from = meet(climb_away, 1)
    climb, climb_away = joined(climb, climb_from)
    fall = settle(fall, fall_away)
    keep, send = back(after(hidden_grad, climb_away, fall), whole_up)
    from_core = over_cores(send)
    far_grad = (keep[1].astype(F32) + from_core[1].astype(F32)).astype(BF16)
    from_pair = over_pair(far_grad)
    climb = settle(climb, climb_away)
    near_grad = after(keep[0].astype(F32) + from_core[0].astype(F32), climb)
    own_pooled = lax.dynamic_slice_in_dim(pooled, core * mine, mine, 0).astype(F32)[:, None, :] / spots
    grad_half = tail(base, live_tiles, near_grad, from_pair, normal, inv, token_grad, own_pooled, dw_kernel, ln_gain)
    other_half = over_cores(grad_half)
    first = jnp.where(core == 0, grad_half, other_half)
    second = jnp.where(core == 0, other_half, grad_half)
    tile_grad = jnp.concatenate([first, second], axis=0)
    grad_down = both_sides(fall, grad_half)
    return (tile_grad, both_sides(climb, tile_grad, grad_down), grad_down)


def solution(mesh):
    sizes = (mesh.shape["seq"], mesh.shape["dp"])
    return jax.shard_map(
        functools.partial(on_device, sizes),
        mesh=mesh,
        in_specs=(
            P(("groups", "seq", "dp"), None, None, None),
            P(("groups", "seq", "dp"), None, None, None),
            P("dp", "groups", "seq"),
            P(("groups", "seq", "dp")),
            P(),
            P(),
            P(),
            P(),
            P("seq", "mp"),
            P("mp"),
            P("seq", "mp"),
            P(),
        ),
        out_specs=(
            P(("groups", "seq", "dp"), None, None, None),
            P(("groups", "seq"), "mp"),
            P(("groups", "seq"), "mp"),
        ),
        check_vma=False,
    )
```
